32 devices in a mesh: span: 8 (over z, x), chord: 4 (over y, core).
Axes of the slice: x: 2, y: 2, z: 4, core: 2. Of those that a mesh axis runs over, the one named last changes fastest.
Arguments:
- pressure: float32 [2, 1024, 512], P(None, 'span', 'chord'), may hold values from 0 to 1
- fill_state: int32 [2, 1024, 512], P(None, 'span', 'chord'), may hold values from 0 to 2
- perm_class: int32 [2, 1024, 512], P(None, 'span', 'chord'), may hold values from 0 to 7
- perm_table: float32 [2, 8], replicated, may hold values from 1 to 4
- inlet_span: int32 [128], replicated, may hold values from 0 to 1023
- inlet_chord: int32 [128], replicated, may hold values from 0 to 511
- inlet_rate: float32 [128], replicated, may hold values from 500 to 1500
Outputs:
- pressure_out: float32 [2, 1024, 512], P(None, 'span', 'chord')
The draws below stay inside these ranges and needn't reach their ends.
Inputs may be any that keep to these rules, and one draw needn't show every extreme that they name: `inlet_span`: inlet cells may repeat; their rates add.
All inputs are finite; a program needn't handle non-finite values.
Results may differ from the reference program's by a relative error of at most 0.00035.
Values sent between devices are 32-bit elements; how exact they have to be, the bound alone decides.
A program may use at most 64 MiB of HBM per device.

```python
import math
import jax
import jax.numpy as jnp

PLIES = 2
STEPS = 1
NCLASS = 8
NIN = 128
NS = 1024
NC = 512


def plant(result, own_key, least, high):
    shape = result.shape
    index_at = [jax.random.randint(jax.random.fold_in(own_key, axis), (), 0, shape[axis]) for axis in range(len(shape))]
    result = result.at[tuple(index_at)].set(least)
    longest = shape.index(max(shape))
    index_at[longest] = (index_at[longest] + 1) % shape[longest]
    return result.at[tuple(index_at)].set(high)


def block_scale(rng, extent, cuts, smallest, high):
    def one(axis_at, blocks):
        steps = jax.random.uniform(jax.random.fold_in(jax.random.fold_in(rng, 6), axis_at), (blocks,), jnp.float32, smallest / len(cuts), high / len(cuts))
        return jnp.repeat(jnp.exp(steps), extent[axis_at] // blocks).reshape((-1,) + (1,) * (len(extent) - axis_at - 1))

    loudness = one(*cuts[0])
    for cut in cuts[1:]:
        loudness = loudness * one(*cut)
    return loudness


def setup_inputs(seed: int = 0) -> dict:
    key_of = jax.random.split(jax.random.key(seed), 8)
    pressure = jnp.clip(1.0 * jax.random.uniform(key_of[0], (PLIES, NS, NC), jnp.float32) ** block_scale(key_of[0], (PLIES, NS, NC), ((1, 8), (2, 4)), -0.2, 0.2), 0.0, 1.0)
    fill_state = plant(jax.random.randint(key_of[1], (PLIES, NS, NC), 0, 3), jax.random.fold_in(key_of[1], 1), 0, 2).astype(jnp.int32)
    perm_class = plant(jax.random.randint(key_of[2], (PLIES, NS, NC), 0, NCLASS), jax.random.fold_in(key_of[2], 1), 0, NCLASS - 1).astype(jnp.int32)
    perm_table = jnp.clip(jnp.exp(jax.random.uniform(key_of[3], (PLIES, NCLASS), jnp.float32, math.log(1.0), math.log(4.0))), 1.0, 4.0)
    inlet_span = plant(jax.random.randint(key_of[4], (NIN,), 0, NS), jax.random.fold_in(key_of[4], 1), 0, NS - 1).astype(jnp.int32)
    inlet_chord = plant(jax.random.randint(key_of[5], (NIN,), 0, NC), jax.random.fold_in(key_of[5], 1), 0, NC - 1).astype(jnp.int32)
    inlet_rate = jnp.clip(jax.random.uniform(key_of[6], (NIN,), jnp.float32, 500.0, 1500.0), 500.0, 1500.0)
    return {"pressure": pressure, "fill_state": fill_state, "perm_class": perm_class, "perm_table": perm_table, "inlet_span": inlet_span, "inlet_chord": inlet_chord, "inlet_rate": inlet_rate}


HALF_RATE = 200.0
COUPLE = 0.3


def shift_lower(values, stride):
    padding = jnp.zeros(values.shape[:-1] + (stride,), values.dtype)
    return jnp.concatenate([padding, values[..., :-stride]], axis=-1)


def shift_upper(values, stride):
    padding = jnp.zeros(values.shape[:-1] + (stride,), values.dtype)
    return jnp.concatenate([values[..., stride:], padding], axis=-1)


def faces(cond):
    summed = HALF_RATE * (cond + shift_upper(cond, 1))
    closing = jnp.zeros(cond.shape[:-1] + (1,), cond.dtype)
    return jnp.concatenate([summed[..., :-1], closing], axis=-1)


def parallel_cyclic_reduction_update(lower_band, diagonal_terms, upper_band, right_hand_side, previous_neighbour_row, next_neighbour_row):
    new_lower = -lower_band * previous_neighbour_row[0]
    new_diag = diagonal_terms - lower_band * previous_neighbour_row[1] - upper_band * next_neighbour_row[0]
    new_upper = -upper_band * next_neighbour_row[1]
    new_rhs = right_hand_side - lower_band * previous_neighbour_row[2] - upper_band * next_neighbour_row[2]
    return new_lower, new_diag, new_upper, new_rhs


def line_solve(lower_band, diagonal_terms, upper_band, right_hand_side):
    total = right_hand_side.shape[-1]
    stride = 1
    while stride < total:
        ratios = (lower_band / diagonal_terms, upper_band / diagonal_terms, right_hand_side / diagonal_terms)
        previous_neighbour_row = [shift_lower(v, stride) for v in ratios]
        next_neighbour_row = [shift_upper(v, stride) for v in ratios]
        lower_band, diagonal_terms, upper_band, right_hand_side = parallel_cyclic_reduction_update(lower_band, diagonal_terms, upper_band, right_hand_side, previous_neighbour_row, next_neighbour_row)
        stride = stride * 2
    return right_hand_side / diagonal_terms


def explicit_core(field, field_next, field_prev, faces_here, faces_prev, source):
    flux = faces_here * (field_next - field) - faces_prev * (field - field_prev)
    return field + flux + COUPLE * (jnp.flip(field, 0) - field) + source


def second_half(star, half_lines, source):
    return 2.0 * star - half_lines + COUPLE * (jnp.flip(star, 0) - star) + source


def reference(pressure, fill_state, perm_class, perm_table, inlet_span, inlet_chord, inlet_rate):
    mobility = jnp.where(fill_state == 0, 1.0, jnp.where(fill_state == 1, 0.5, 0.25))
    plies_idx = jnp.arange(PLIES, dtype=jnp.int32)[:, None, None]
    cond = perm_table[plies_idx, perm_class] * mobility
    plane = jnp.zeros((NS, NC), jnp.float32).at[inlet_span, inlet_chord].add(inlet_rate)
    source = jnp.broadcast_to(plane[None], (PLIES, NS, NC))
    source_turned = jnp.transpose(source, (0, 2, 1))
    chord_faces = faces(cond)
    chord_prev = shift_lower(chord_faces, 1)
    span_faces = faces(jnp.transpose(cond, (0, 2, 1)))
    span_prev = shift_lower(span_faces, 1)
    field = pressure
    for step in range(STEPS):
        half = explicit_core(field, shift_upper(field, 1), shift_lower(field, 1), chord_faces, chord_prev, source)
        half_turned = jnp.transpose(half, (0, 2, 1))
        star = line_solve(-span_prev, 1.0 + span_prev + span_faces, -span_faces, half_turned)
        second = second_half(star, half_turned, source_turned)
        field = line_solve(-chord_prev, 1.0 + chord_prev + chord_faces, -chord_faces, jnp.transpose(second, (0, 2, 1)))
    return field
```

```python
import functools

import jax
import jax.numpy as jnp
from jax import lax
from jax.experimental import pallas as pl
from jax.experimental.pallas import tpu as pltpu
from jax.sharding import PartitionSpec as P

HALF_RATE = 200.0
COUPLE = 0.3
MESH = pl.DeviceIdType.MESH
TILE = 8
LIMIT = 16 << 20


def down(x, s):
    if s % TILE == 0:
        return jnp.concatenate([x[-s:], x[:-s]], axis=0)
    return pltpu.roll(x, s, 0)


def up(x, s):
    if s % TILE == 0:
        return jnp.concatenate([x[s:], x[:s]], axis=0)
    return pltpu.roll(x, x.shape[0] - s, 0)


def from_row(s, value, other):
    if s % TILE == 0:
        return jnp.concatenate([other[:s], value[s:]], axis=0)
    rows = lax.broadcasted_iota(jnp.int32, value.shape, 0)
    return jnp.where(rows >= s, value, other)


def to_row(s, value, other):
    n = value.shape[0]
    if s % TILE == 0:
        return jnp.concatenate([value[: n - s], other[n - s :]], axis=0)
    rows = lax.broadcasted_iota(jnp.int32, value.shape, 0)
    return jnp.where(rows < n - s, value, other)


def factor(cond, keep):
    n = cond.shape[0]
    zero = jnp.zeros_like(cond)
    one = jnp.ones_like(cond)
    g = HALF_RATE * (cond + up(cond, 1))
    a = from_row(1, down(g, 1), one)
    c = to_row(1, g, one)
    e = one
    s, k = 1, 0
    while s < n:
        a_in = from_row(s, a, zero)
        c_in = to_row(s, c, zero)
        rb = 1.0 / (e + a_in + c_in)
        al = a_in * down(rb, s)
        be = c_in * up(rb, s)
        keep(k, al, be)
        a = from_row(s, al * down(a, s), a)
        c = to_row(s, be * up(c, s), c)
        e = e + al * down(e, s) + be * up(e, s)
        s, k = 2 * s, k + 1
    re = 1.0 / e
    return a * re, c * re, re


def reduce_rhs(d, kept, re):
    n = d.shape[0]
    s, k = 1, 0
    while s < n:
        al, be = kept(k)
        if s % TILE == 0:
            zero = jnp.zeros_like(d[:s])
            d = (
                d
                + jnp.concatenate([zero, al[s:] * d[:-s]], axis=0)
                + jnp.concatenate([be[:-s] * d[s:], zero], axis=0)
            )
        else:
            d = d + al * down(d, s) + be * up(d, s)
        s, k = 2 * s, k + 1
    return d * re


class Gather:
    def __init__(self, axis, n, me, buf, send, recv):
        self.copies = []
        for o in range(1, n):
            dst = lax.rem(me + o, n)
            self.copies.append(
                pltpu.make_async_remote_copy(buf.at[me], buf.at[me], send, recv, {axis: dst}, MESH)
            )
        many = buf.at[pl.ds(0, n - 1)]
        self.all = pltpu.make_async_remote_copy(many, many, send, recv, {axis: lax.rem(me + 1, n)}, MESH)

    def start(self):
        for copy in self.copies:
            copy.start()

    def wait(self):
        self.all.wait_recv()

    def wait_sent(self):
        self.all.wait_send()


def put_coefs(buf, me, plies, p, A, C, cond):
    n = A.shape[0]
    values = (A[:1], C[n - 1 :], A[n - 1 :], cond[:1], cond[n - 1 :])
    for q, v in enumerate(values):
        buf[me, q * plies + p : q * plies + p + 1, :] = v


def flux_factor(buf, n, plies):
    def at(j, q):
        return buf[j, q * plies : (q + 1) * plies, :]

    w, m = [None] * (n + 1), [None] * (n + 1)
    cross = [at(j, 2) for j in range(n)]
    for j in range(1, n):
        diag = 1.0 / (HALF_RATE * (at(j - 1, 4) + at(j, 3))) + at(j - 1, 1) + at(j, 0)
        if j > 1:
            m[j] = cross[j - 1] * w[j - 1]
            diag = diag - cross[j - 1] * m[j]
        w[j] = 1.0 / diag
    return w, m, cross


def flux_solve(buf, n, plies, me, w, m, cross):
    y = [None] * (n + 1)
    for j in range(1, n):
        r = buf[j - 1, plies : 2 * plies, :] - buf[j, :plies, :]
        y[j] = r if j == 1 else r + m[j] * y[j - 1]
    zero = jnp.zeros((plies, buf.shape[-1]), jnp.float32)
    top, bottom = zero, zero
    flux = None
    for j in range(n - 1, 0, -1):
        flux = w[j] * (y[j] if flux is None else y[j] + cross[j] * flux)
        top = jnp.where(me == j, flux, top)
        bottom = jnp.where(me + 1 == j, flux, bottom)
    return top, bottom


def kernel(
    ns, nc, plies, classes,
    pressure_hbm, fill_hbm, class_hbm, table_hbm, span_hbm, chord_hbm, rate_hbm,
    D_c, A_c, C_c, flux_ref,
    pressure, state, table_ref, inlet_ref, rate_ref, half, keep_s, keep_c, A_s, C_s, E_s, E_c, D, sides,
    halo_out, halo_in, coef_s, coef_c, edge_s, edge_c,
    sent, landed,
):
    rows, width = pressure.shape[1:]
    me_s, me_c = lax.axis_index("span"), lax.axis_index("chord")
    barrier = pltpu.get_barrier_semaphore()
    for o in range(1, nc):
        pl.semaphore_signal(
            barrier, inc=1, device_id={"chord": lax.rem(me_c + o, nc)}, device_id_type=MESH
        )
    loads = [
        pltpu.make_async_copy(src, dst, sent.at[i])
        for src, dst, i in (
            (class_hbm, state.at[0], 0), (fill_hbm, state.at[1], 0), (pressure_hbm, pressure, 1),
            (table_hbm, table_ref, 2), (span_hbm, inlet_ref.at[0], 3), (chord_hbm, inlet_ref.at[1], 3),
            (rate_hbm, rate_ref, 4),
        )
    ]
    for load in loads:
        load.start()
    for o in range(1, ns):
        pl.semaphore_signal(
            barrier, inc=1, device_id={"span": lax.rem(me_s + o, ns)}, device_id_type=MESH
        )

    pltpu.make_async_copy(state, state, sent.at[0]).wait()
    pltpu.make_async_copy(pressure, pressure, sent.at[1]).wait()
    loads[3].wait()
    pltpu.make_async_copy(inlet_ref, inlet_ref, sent.at[3]).wait()
    loads[6].wait()

    conds, turned, fields = [], [], []
    for p in range(plies):
        perm = jnp.full((rows, width), table_ref[p, 0], jnp.float32)
        kl = state[0, p]
        for k in range(1, classes):
            perm = jnp.where(kl == k, table_ref[p, k], perm)
        st = state[1, p]
        cond = perm * jnp.where(st == 0, 1.0, jnp.where(st == 1, 0.5, 0.25))
        conds.append(cond)
        turned.append(cond.T)
        fields.append(pressure[p].T)
        for side, at in ((0, 0), (1, width - 1)):
            halo_out[side, p : p + 1, :] = turned[p][at : at + 1]
            halo_out[side, plies + p : plies + p + 1, :] = fields[p][at : at + 1]

    pl.semaphore_wait(barrier, ns + nc - 2)
    ahead, behind = lax.rem(me_c + 1, nc), lax.rem(me_c + nc - 1, nc)
    halos = [
        pltpu.make_async_remote_copy(
            halo_out.at[side], halo_in.at[side], sent.at[0], landed.at[0],
            {"chord": to}, MESH,
        )
        for side, to in ((0, behind), (1, ahead))
    ]
    for copy in halos:
        copy.start()
    both = pltpu.make_async_remote_copy(
        halo_out, halo_in, sent.at[0], landed.at[0], {"chord": ahead}, MESH
    )

    def keeper(ref, p):
        def keep(k, al, be):
            ref[k, 0, p] = al
            ref[k, 1, p] = be

        return keep

    def kept(ref, p):
        return lambda k: (ref[k, 0, p], ref[k, 1, p])

    for p in range(plies):
        A, C, re = factor(conds[p], keeper(keep_s, p))
        A_s[p], C_s[p], E_s[p] = A, C, re
        put_coefs(coef_s, me_s, plies, p, A, C, conds[p])
    span_coefs = Gather("span", ns, me_s, coef_s, sent.at[1], landed.at[1])
    span_coefs.start()

    row_id = lax.broadcasted_iota(jnp.int32, (rows, rate_ref.shape[1]), 0) + me_s * rows
    col_id = lax.broadcasted_iota(jnp.int32, (width, rate_ref.shape[1]), 0) + me_c * width
    row_hits = jnp.where(row_id == inlet_ref[0], rate_ref[...], 0.0)
    col_hits = jnp.where(col_id == inlet_ref[1], 1.0, 0.0)
    plane = lax.dot_general(
        row_hits, col_hits, (((1,), (1,)), ((), ())),
        precision=lax.Precision.HIGHEST, preferred_element_type=jnp.float32,
    )

    explicit = []
    for p in range(plies):
        f, other = fields[p], fields[plies - 1 - p]
        g = HALF_RATE * (turned[p] + up(turned[p], 1))
        flow = to_row(1, g * (up(f, 1) - f), jnp.zeros_like(f))
        back = from_row(1, down(flow, 1), jnp.zeros_like(f))
        explicit.append(f + (flow - back) + COUPLE * (other - f))

    for p in range(plies):
        rhs = explicit[p].T + plane
        half[p] = rhs
        d = reduce_rhs(rhs, kept(keep_s, p), E_s[p])
        edge_s[me_s, p : p + 1, :] = d[:1]
        edge_s[me_s, plies + p : plies + p + 1, :] = d[rows - 1 :]
        for q, response in enumerate((A_s[p].T, C_s[p].T)):
            sides[2 * q, p : p + 1, :] = response[:1]
            sides[2 * q + 1, p : p + 1, :] = response[width - 1 :]

    both.wait_recv()

    def inflow(mine, theirs):
        conds_sum = halo_in[theirs, :plies, :] + halo_out[mine, :plies, :]
        return HALF_RATE * conds_sum * (halo_in[theirs, plies:, :] - halo_out[mine, plies:, :])

    first = jnp.where(me_c > 0, inflow(0, 1), 0.0)
    last = jnp.where(me_c < nc - 1, inflow(1, 0), 0.0)
    lane = lax.broadcasted_iota(jnp.int32, (plies, width), 1)
    for q in range(2):
        by_first = jnp.sum(sides[2 * q] * first, axis=1, keepdims=True)
        by_last = jnp.sum(sides[2 * q + 1] * last, axis=1, keepdims=True)
        edge_s[me_s, q * plies : (q + 1) * plies, :] = (
            edge_s[me_s, q * plies : (q + 1) * plies, :]
            + jnp.where(lane == 0, by_first, 0.0)
            + jnp.where(lane == width - 1, by_last, 0.0)
        )
    span_edges = Gather("span", ns, me_s, edge_s, sent.at[3], landed.at[3])
    span_edges.start()

    lanes = lax.broadcasted_iota(jnp.int32, (width, rows), 0)
    for p in range(plies):
        change = jnp.where(lanes == 0, first[p : p + 1], 0.0) + jnp.where(
            lanes == width - 1, last[p : p + 1], 0.0
        )
        rhs = half[p] + change.T
        half[p] = rhs
        D[p] = reduce_rhs(rhs, kept(keep_s, p), E_s[p])

    for p in range(plies):
        A, C, re = factor(turned[p], keeper(keep_c, p))
        A_c[p], C_c[p], E_c[p] = A, C, re
        put_coefs(coef_c, me_c, plies, p, A, C, turned[p])
    chord_coefs = Gather("chord", nc, me_c, coef_c, sent.at[2], landed.at[2])
    chord_coefs.start()

    span_coefs.wait()
    parts = flux_factor(coef_s, ns, plies)
    span_edges.wait()
    top, bottom = flux_solve(edge_s, ns, plies, me_s, *parts)
    stars = [D[p] + A_s[p] * top[p : p + 1] - C_s[p] * bottom[p : p + 1] for p in range(plies)]
    for p in range(plies):
        star, other = stars[p], stars[plies - 1 - p]
        second = 2.0 * star - half[p] + COUPLE * (other - star) + plane
        d = reduce_rhs(second.T, kept(keep_c, p), E_c[p])
        D_c[p] = d
        edge_c[me_c, p : p + 1, :] = d[:1]
        edge_c[me_c, plies + p : plies + p + 1, :] = d[width - 1 :]
    chord_edges = Gather("chord", nc, me_c, edge_c, sent.at[4], landed.at[4])
    chord_edges.start()

    chord_coefs.wait()
    parts = flux_factor(coef_c, nc, plies)
    both.wait_send()
    for gather in (span_coefs, chord_coefs, span_edges):
        gather.wait_sent()
    chord_edges.wait()
    flux_ref[0], flux_ref[1] = flux_solve(edge_c, nc, plies, me_c, *parts)
    chord_edges.wait_sent()


def finish(plies, D_c, A_c, C_c, flux_ref, out_hbm, block, sem):
    copies = []
    for p in range(plies):
        top, bottom = flux_ref[0, p : p + 1, :], flux_ref[1, p : p + 1, :]
        block[p] = (D_c[p] + A_c[p] * top - C_c[p] * bottom).T
        copies.append(pltpu.make_async_copy(block.at[p], out_hbm.at[p], sem.at[p]))
        copies[-1].start()
    for copy in copies:
        copy.wait()


def levels(n):
    return max(1, (n - 1).bit_length())


def per_device(ns, nc, pressure, fill_state, perm_class, perm_table, inlet_span, inlet_chord, inlet_rate):
    plies, rows, width = pressure.shape
    classes = perm_table.shape[1]
    inlets = inlet_span.shape[0]
    vmem = pl.BlockSpec(memory_space=pltpu.VMEM)
    hbm = pl.BlockSpec(memory_space=pltpu.HBM)
    f32 = jnp.float32
    block = pltpu.VMEM((plies, rows, width), f32)
    block_t = pltpu.VMEM((plies, width, rows), f32)
    iblock = pltpu.VMEM((plies, rows, width), jnp.int32)
    dma = lambda n: pltpu.SemaphoreType.DMA((n,))
    lines = pltpu.VMEM((plies, width, rows), f32)
    solved = pl.pallas_call(
        functools.partial(kernel, ns, nc, plies, classes),
        out_shape=(lines, lines, lines, pltpu.VMEM((2, plies, rows), f32)),
        in_specs=[hbm] * 7,
        out_specs=(vmem,) * 4,
        scratch_shapes=[
            block, pltpu.VMEM((2, plies, rows, width), jnp.int32),
            pltpu.SMEM(perm_table.shape, f32),
            pltpu.VMEM((2, 1, inlets), jnp.int32), pltpu.VMEM((1, inlets), f32),
            block,
            pltpu.VMEM((levels(rows), 2, plies, rows, width), f32),
            pltpu.VMEM((levels(width), 2, plies, width, rows), f32),
            block, block, block, block_t, block,
            pltpu.VMEM((4, plies, rows), f32),
            pltpu.VMEM((2, 2 * plies, rows), f32),
            pltpu.VMEM((2, 2 * plies, rows), f32),
            pltpu.VMEM((ns, 5 * plies, width), f32),
            pltpu.VMEM((nc, 5 * plies, rows), f32),
            pltpu.VMEM((ns, 2 * plies, width), f32),
            pltpu.VMEM((nc, 2 * plies, rows), f32),
            dma(5), dma(5),
        ],
        compiler_params=pltpu.CompilerParams(collective_id=0, has_side_effects=True, vmem_limit_bytes=LIMIT),
    )(
        *(
            pltpu.with_memory_space_constraint(x, pltpu.HBM)
            for x in (
                pressure, fill_state, perm_class, perm_table, inlet_span.reshape(1, inlets),
                inlet_chord.reshape(1, inlets), inlet_rate.reshape(1, inlets),
            )
        )
    )
    return pl.pallas_call(
        functools.partial(finish, plies),
        out_shape=jax.ShapeDtypeStruct(pressure.shape, f32),
        in_specs=[vmem] * 4,
        out_specs=hbm,
        scratch_shapes=[block, dma(plies)],
        compiler_params=pltpu.CompilerParams(vmem_limit_bytes=LIMIT),
    )(*solved)


def solution(mesh):
    block = P(None, "span", "chord")
    return jax.shard_map(
        functools.partial(per_device, mesh.shape["span"], mesh.shape["chord"]),
        mesh=mesh,
        in_specs=(block, block, block, P(), P(), P(), P()),
        out_specs=block,
        check_vma=False,
    )
```

```python
import functools

import jax
import jax.numpy as jnp
from jax import lax
from jax.experimental import pallas as pl
from jax.experimental.pallas import tpu as pltpu
from jax.sharding import PartitionSpec as P

HALF_RATE = 200.0
COUPLE = 0.3
MESH = pl.DeviceIdType.MESH
TILE = 8
LIMIT = 16 << 20


def down(x, s):
    if s % TILE == 0:
        return jnp.concatenate([x[-s:], x[:-s]], axis=0)
    return pltpu.roll(x, s, 0)


def up(x, s):
    if s % TILE == 0:
        return jnp.concatenate([x[s:], x[:s]], axis=0)
    return pltpu.roll(x, x.shape[0] - s, 0)


def from_row(s, value, other):
    if s % TILE == 0:
        return jnp.concatenate([other[:s], value[s:]], axis=0)
    rows = lax.broadcasted_iota(jnp.int32, value.shape, 0)
    return jnp.where(rows >= s, value, other)


def to_row(s, value, other):
    n = value.shape[0]
    if s % TILE == 0:
        return jnp.concatenate([value[: n - s], other[n - s :]], axis=0)
    rows = lax.broadcasted_iota(jnp.int32, value.shape, 0)
    return jnp.where(rows < n - s, value, other)


def factor(cond, keep):
    n = cond.shape[0]
    zero = jnp.zeros_like(cond)
    one = jnp.ones_like(cond)
    g = HALF_RATE * (cond + up(cond, 1))
    a = from_row(1, down(g, 1), one)
    c = to_row(1, g, one)
    e = one
    s, k = 1, 0
    while s < n:
        a_in = from_row(s, a, zero)
        c_in = to_row(s, c, zero)
        rb = 1.0 / (e + a_in + c_in)
        al = a_in * down(rb, s)
        be = c_in * up(rb, s)
        keep(k, al, be)
        a = from_row(s, al * down(a, s), a)
        c = to_row(s, be * up(c, s), c)
        e = e + al * down(e, s) + be * up(e, s)
        s, k = 2 * s, k + 1
    re = 1.0 / e
    return a * re, c * re, re


def reduce_rhs(d, kept, re):
    n = d.shape[0]
    s, k = 1, 0
    while s < n:
        al, be = kept(k)
        if s % TILE == 0:
            zero = jnp.zeros_like(d[:s])
            d = (
                d
                + jnp.concatenate([zero, al[s:] * d[:-s]], axis=0)
                + jnp.concatenate([be[:-s] * d[s:], zero], axis=0)
            )
        else:
            d = d + al * down(d, s) + be * up(d, s)
        s, k = 2 * s, k + 1
    return d * re


def others(n, me):
    return [k + (me <= k).astype(jnp.int32) for k in range(n - 1)]


class Gather:
    def __init__(self, axis, n, me, buf, send, recv):
        targets = others(n, me)
        self.copies = [
            pltpu.make_async_remote_copy(buf.at[me], buf.at[me], send, recv, {axis: to}, MESH)
            for to in targets
        ]
        many = buf.at[pl.ds(0, n - 1)]
        self.all = pltpu.make_async_remote_copy(many, many, send, recv, {axis: targets[0]}, MESH)

    def start(self):
        for copy in self.copies:
            copy.start()

    def wait(self):
        self.all.wait_recv()

    def wait_sent(self):
        self.all.wait_send()


def put_coefs(buf, me, plies, p, A, C, cond):
    n = A.shape[0]
    values = (A[:1], C[n - 1 :], A[n - 1 :], cond[:1], cond[n - 1 :])
    for q, v in enumerate(values):
        buf[me, q * plies + p : q * plies + p + 1, :] = v


def flux_factor(buf, n, plies):
    def at(j, q):
        return buf[j, q * plies : (q + 1) * plies, :]

    w, m = [None] * (n + 1), [None] * (n + 1)
    cross = [at(j, 2) for j in range(n)]
    for j in range(1, n):
        diag = 1.0 / (HALF_RATE * (at(j - 1, 4) + at(j, 3))) + at(j - 1, 1) + at(j, 0)
        if j > 1:
            m[j] = cross[j - 1] * w[j - 1]
            diag = diag - cross[j - 1] * m[j]
        w[j] = 1.0 / diag
    return w, m, cross


def flux_solve(buf, n, plies, me, w, m, cross, fix=None):
    y = [None] * (n + 1)
    for j in range(1, n):
        r = buf[j - 1, plies : 2 * plies, :] - buf[j, :plies, :]
        if fix is not None:
            r = r + fix[j]
        y[j] = r if j == 1 else r + m[j] * y[j - 1]
    zero = jnp.zeros((plies, buf.shape[-1]), jnp.float32)
    top, bottom = zero, zero
    flux = None
    for j in range(n - 1, 0, -1):
        flux = w[j] * (y[j] if flux is None else y[j] + cross[j] * flux)
        top = jnp.where(me == j, flux, top)
        bottom = jnp.where(me + 1 == j, flux, bottom)
    return top, bottom


def kernel(
    ns, nc, plies, classes,
    pressure_hbm, fill_hbm, class_hbm, table_hbm, span_hbm, chord_hbm, rate_hbm,
    D_c, A_c, C_c, flux_ref,
    pressure, state, table_ref, inlet_ref, rate_ref, plane_ref, half, keep_s, keep_c, A_s, C_s, E_s, E_c, D,
    sides, near_out, near_in, cross_out, cross_in, coef_s, coef_c, edge_s, edge_c,
    sent, landed,
):
    rows, width = pressure.shape[1:]
    me_s, me_c = lax.axis_index("span"), lax.axis_index("chord")
    odd = lax.rem(me_c, 2)
    beside = me_c + 1 - 2 * odd
    across = lax.rem(me_c + nc - 1 + 2 * odd, nc)
    is_odd = odd == 1
    has_across = jnp.where(is_odd, me_c < nc - 1, me_c > 0)
    lane_beside = (1 - odd) * (width - 1)
    lane_across = odd * (width - 1)

    barrier = pltpu.get_barrier_semaphore()
    loads = [
        pltpu.make_async_copy(src, dst, sent.at[i])
        for src, dst, i in (
            (span_hbm, inlet_ref.at[0], 3), (chord_hbm, inlet_ref.at[1], 3), (rate_hbm, rate_ref, 4),
            (table_hbm, table_ref, 2), (class_hbm, state.at[0], 0), (fill_hbm, state.at[1], 0),
            (pressure_hbm, pressure, 1),
        )
    ]
    for load in loads:
        load.start()
    for o in range(1, nc):
        pl.semaphore_signal(
            barrier, inc=1, device_id={"chord": lax.rem(me_c + o, nc)}, device_id_type=MESH
        )
    for to in others(ns, me_s):
        pl.semaphore_signal(barrier, inc=1, device_id={"span": to}, device_id_type=MESH)
        pl.semaphore_signal(
            barrier, inc=1, device_id={"span": to, "chord": across}, device_id_type=MESH
        )

    pltpu.make_async_copy(inlet_ref, inlet_ref, sent.at[3]).wait()
    loads[2].wait()
    row_id = lax.broadcasted_iota(jnp.int32, (rows, rate_ref.shape[1]), 0) + me_s * rows
    col_id = lax.broadcasted_iota(jnp.int32, (width, rate_ref.shape[1]), 0) + me_c * width
    row_hits = jnp.where(row_id == inlet_ref[0], rate_ref[...], 0.0)
    col_hits = jnp.where(col_id == inlet_ref[1], 1.0, 0.0)
    plane_ref[...] = lax.dot_general(
        row_hits, col_hits, (((1,), (1,)), ((), ())),
        precision=lax.Precision.HIGHEST, preferred_element_type=jnp.float32,
    )
    loads[3].wait()
    pltpu.make_async_copy(state, state, sent.at[0]).wait()
    pltpu.make_async_copy(pressure, pressure, sent.at[1]).wait()

    conds, turned, fields = [], [], []
    for p in range(plies):
        perm = jnp.full((rows, width), table_ref[p, 0], jnp.float32)
        kl = state[0, p]
        for k in range(1, classes):
            perm = jnp.where(kl == k, table_ref[p, k], perm)
        st = state[1, p]
        cond = perm * jnp.where(st == 0, 1.0, jnp.where(st == 1, 0.5, 0.25))
        conds.append(cond)
        turned.append(cond.T)
        fields.append(pressure[p].T)
        for q, v in ((p, turned[p]), (plies + p, fields[p])):
            head, tail = v[:1], v[width - 1 :]
            near_out[q : q + 1, :] = jnp.where(is_odd, head, tail)
            cross_out[q : q + 1, :] = jnp.where(is_odd, tail, head)
    pl.semaphore_wait(barrier, 2 * (ns - 1) + nc - 1)
    near = pltpu.make_async_remote_copy(
        near_out, near_in, sent.at[0], landed.at[0], {"chord": beside}, MESH
    )
    near.start()
    mine = pltpu.make_async_remote_copy(
        cross_out, cross_in.at[me_s], sent.at[1], landed.at[1], {"chord": across}, MESH
    )
    mine.start()
    for to in others(ns, me_s):
        pltpu.make_async_remote_copy(
            cross_out, cross_in.at[me_s], sent.at[1], landed.at[2], {"span": to, "chord": across}, MESH
        ).start()

    def keeper(ref, p):
        def keep(k, al, be):
            ref[k, 0, p] = al
            ref[k, 1, p] = be

        return keep

    def kept(ref, p):
        return lambda k: (ref[k, 0, p], ref[k, 1, p])

    def put(q, p, v):
        coef_s[me_s, q * plies + p : q * plies + p + 1, :] = v

    for p in range(plies):
        A, C, re = factor(conds[p], keeper(keep_s, p))
        A_s[p], C_s[p], E_s[p] = A, C, re
        put_coefs(coef_s, me_s, plies, p, A, C, conds[p])
        put(5, p, cross_out[p : p + 1, :])
        put(6, p, cross_out[plies + p : plies + p + 1, :])
        for q, response in enumerate((A.T, C.T)):
            head, tail = response[:1], response[width - 1 :]
            put(7 + q, p, jnp.where(is_odd, tail, head))
            sides[q, p : p + 1, :] = jnp.where(is_odd, head, tail)
    span_coefs = Gather("span", ns, me_s, coef_s, sent.at[2], landed.at[3])
    span_coefs.start()

    plane = plane_ref[...]
    for p in range(plies):
        f, other = fields[p], fields[plies - 1 - p]
        g = HALF_RATE * (turned[p] + up(turned[p], 1))
        flow = to_row(1, g * (up(f, 1) - f), jnp.zeros_like(f))
        back = from_row(1, down(flow, 1), jnp.zeros_like(f))
        rhs = (f + (flow - back) + COUPLE * (other - f)).T + plane
        half[p] = rhs
        edge_s[me_s, p : p + 1, :] = jnp.sum(A_s[p] * rhs, axis=0, keepdims=True)
        edge_s[me_s, plies + p : plies + p + 1, :] = jnp.sum(C_s[p] * rhs, axis=0, keepdims=True)
    near.wait_recv()
    near.wait_send()

    def inflow(ours, theirs):
        return (
            HALF_RATE
            * (theirs[:plies] + ours[:plies])
            * (theirs[plies : 2 * plies] - ours[plies : 2 * plies])
        )

    lane = lax.broadcasted_iota(jnp.int32, (plies, width), 1)
    from_beside = inflow(near_out[...], near_in[...])
    for q in range(2):
        change = jnp.sum(sides[q] * from_beside, axis=1, keepdims=True)
        edge_s[me_s, q * plies : (q + 1) * plies, :] = (
            edge_s[me_s, q * plies : (q + 1) * plies, :] + jnp.where(lane == lane_beside, change, 0.0)
        )
    span_edges = Gather("span", ns, me_s, edge_s, sent.at[3], landed.at[4])
    span_edges.start()

    for p in range(plies):
        A, C, re = factor(turned[p], keeper(keep_c, p))
        A_c[p], C_c[p], E_c[p] = A, C, re
        put_coefs(coef_c, me_c, plies, p, A, C, turned[p])
    chord_coefs = Gather("chord", nc, me_c, coef_c, sent.at[4], landed.at[5])
    chord_coefs.start()

    mine.wait_recv()
    from_across = jnp.where(has_across, inflow(cross_out[...], cross_in[me_s]), 0.0)
    lanes = lax.broadcasted_iota(jnp.int32, (width, rows), 0)
    for p in range(plies):
        change = jnp.where(lanes == lane_beside, from_beside[p : p + 1], 0.0) + jnp.where(
            lanes == lane_across, from_across[p : p + 1], 0.0
        )
        rhs = half[p] + change.T
        half[p] = rhs
        D[p] = reduce_rhs(rhs, kept(keep_s, p), E_s[p])

    few = cross_in.at[pl.ds(0, ns - 1)]
    pltpu.make_async_remote_copy(few, few, sent.at[1], landed.at[2], {"chord": across}, MESH).wait_recv()
    span_coefs.wait()
    parts = flux_factor(coef_s, ns, plies)
    by_first, by_last = [], []
    for i in range(ns):
        ours = coef_s[i, 5 * plies : 7 * plies, :]
        flow = jnp.where(has_across, inflow(ours, cross_in[i]), 0.0)
        by_first.append(jnp.sum(coef_s[i, 7 * plies : 8 * plies, :] * flow, axis=1, keepdims=True))
        by_last.append(jnp.sum(coef_s[i, 8 * plies : 9 * plies, :] * flow, axis=1, keepdims=True))
    fix = [None] + [
        jnp.where(lane == lane_across, by_last[i - 1] - by_first[i], 0.0) for i in range(1, ns)
    ]
    span_edges.wait()
    top, bottom = flux_solve(edge_s, ns, plies, me_s, *parts, fix)
    plane = plane_ref[...]
    stars = [D[p] + A_s[p] * top[p : p + 1] - C_s[p] * bottom[p : p + 1] for p in range(plies)]
    seconds = []
    for p in range(plies):
        star, other = stars[p], stars[plies - 1 - p]
        second = (2.0 * star - half[p] + COUPLE * (other - star) + plane).T
        seconds.append(second)
        edge_c[me_c, p : p + 1, :] = jnp.sum(A_c[p] * second, axis=0, keepdims=True)
        edge_c[me_c, plies + p : plies + p + 1, :] = jnp.sum(C_c[p] * second, axis=0, keepdims=True)
    chord_edges = Gather("chord", nc, me_c, edge_c, sent.at[0], landed.at[6])
    chord_edges.start()
    for p in range(plies):
        D_c[p] = reduce_rhs(seconds[p], kept(keep_c, p), E_c[p])

    chord_coefs.wait()
    parts = flux_factor(coef_c, nc, plies)
    pltpu.make_async_remote_copy(cross_in, cross_in, sent.at[1], landed.at[2], {"chord": across}, MESH).wait_send()
    for gather in (span_coefs, chord_coefs, span_edges):
        gather.wait_sent()
    chord_edges.wait()
    flux_ref[0], flux_ref[1] = flux_solve(edge_c, nc, plies, me_c, *parts)
    chord_edges.wait_sent()


def finish(plies, D_c, A_c, C_c, flux_ref, out_hbm, block, sem):
    for p in range(plies):
        top, bottom = flux_ref[0, p : p + 1, :], flux_ref[1, p : p + 1, :]
        block[p] = (D_c[p] + A_c[p] * top - C_c[p] * bottom).T
        pltpu.make_async_copy(block.at[p], out_hbm.at[p], sem.at[0]).start()
    pltpu.make_async_copy(block, out_hbm, sem.at[0]).wait()


def levels(n):
    return max(1, (n - 1).bit_length())


def per_device(ns, nc, pressure, fill_state, perm_class, perm_table, inlet_span, inlet_chord, inlet_rate):
    plies, rows, width = pressure.shape
    classes = perm_table.shape[1]
    inlets = inlet_span.shape[0]
    vmem = pl.BlockSpec(memory_space=pltpu.VMEM)
    hbm = pl.BlockSpec(memory_space=pltpu.HBM)
    f32 = jnp.float32
    block = pltpu.VMEM((plies, rows, width), f32)
    block_t = pltpu.VMEM((plies, width, rows), f32)
    dma = lambda n: pltpu.SemaphoreType.DMA((n,))
    lines = pltpu.VMEM((plies, width, rows), f32)
    solved = pl.pallas_call(
        functools.partial(kernel, ns, nc, plies, classes),
        out_shape=(lines, lines, lines, pltpu.VMEM((2, plies, rows), f32)),
        in_specs=[hbm] * 7,
        out_specs=(vmem,) * 4,
        scratch_shapes=[
            block, pltpu.VMEM((2, plies, rows, width), jnp.int32),
            pltpu.SMEM(perm_table.shape, f32),
            pltpu.VMEM((2, 1, inlets), jnp.int32), pltpu.VMEM((1, inlets), f32),
            pltpu.VMEM((rows, width), f32),
            block,
            pltpu.VMEM((levels(rows), 2, plies, rows, width), f32),
            pltpu.VMEM((levels(width), 2, plies, width, rows), f32),
            block, block, block, block_t, block,
            pltpu.VMEM((2, plies, rows), f32),
            pltpu.VMEM((2 * plies, rows), f32),
            pltpu.VMEM((2 * plies, rows), f32),
            pltpu.VMEM((2 * plies, rows), f32),
            pltpu.VMEM((ns, 2 * plies, rows), f32),
            pltpu.VMEM((ns, 9 * plies, width), f32),
            pltpu.VMEM((nc, 5 * plies, rows), f32),
            pltpu.VMEM((ns, 2 * plies, width), f32),
            pltpu.VMEM((nc, 2 * plies, rows), f32),
            dma(5), dma(7),
        ],
        compiler_params=pltpu.CompilerParams(collective_id=0, has_side_effects=True, vmem_limit_bytes=LIMIT),
    )(
        *(
            pltpu.with_memory_space_constraint(x, pltpu.HBM)
            for x in (
                pressure, fill_state, perm_class, perm_table, inlet_span.reshape(1, inlets),
                inlet_chord.reshape(1, inlets), inlet_rate.reshape(1, inlets),
            )
        )
    )
    return pl.pallas_call(
        functools.partial(finish, plies),
        out_shape=jax.ShapeDtypeStruct(pressure.shape, f32),
        in_specs=[vmem] * 4,
        out_specs=hbm,
        scratch_shapes=[block, dma(1)],
        compiler_params=pltpu.CompilerParams(vmem_limit_bytes=LIMIT),
    )(*solved)


def solution(mesh):
    block = P(None, "span", "chord")
    return jax.shard_map(
        functools.partial(per_device, mesh.shape["span"], mesh.shape["chord"]),
        mesh=mesh,
        in_specs=(block, block, block, P(), P(), P(), P()),
        out_specs=block,
        check_vma=False,
    )
```

```python
import functools

import jax
import jax.numpy as jnp
from jax import lax
from jax.experimental import pallas as pl
from jax.experimental.pallas import tpu as pltpu
from jax.sharding import PartitionSpec as P

HALF_RATE = 200.0
COUPLE = 0.3
MESH = pl.DeviceIdType.MESH
TILE = 8
LIMIT = 16 << 20


def down(x, s):
    if s % TILE == 0:
        return jnp.concatenate([x[-s:], x[:-s]], axis=0)
    return pltpu.roll(x, s, 0)


def up(x, s):
    if s % TILE == 0:
        return jnp.concatenate([x[s:], x[:s]], axis=0)
    return pltpu.roll(x, x.shape[0] - s, 0)


def from_row(s, value, other):
    if s % TILE == 0:
        return jnp.concatenate([other[:s], value[s:]], axis=0)
    rows = lax.broadcasted_iota(jnp.int32, value.shape, 0)
    return jnp.where(rows >= s, value, other)


def to_row(s, value, other):
    n = value.shape[0]
    if s % TILE == 0:
        return jnp.concatenate([value[: n - s], other[n - s :]], axis=0)
    rows = lax.broadcasted_iota(jnp.int32, value.shape, 0)
    return jnp.where(rows < n - s, value, other)


def factor(cond, keep):
    n = cond.shape[0]
    zero = jnp.zeros_like(cond)
    one = jnp.ones_like(cond)
    g = HALF_RATE * (cond + up(cond, 1))
    a = from_row(1, down(g, 1), one)
    c = to_row(1, g, one)
    e = one
    s, k = 1, 0
    while s < n:
        a_in = from_row(s, a, zero)
        c_in = to_row(s, c, zero)
        rb = 1.0 / (e + a_in + c_in)
        al = a_in * down(rb, s)
        be = c_in * up(rb, s)
        keep(k, al, be)
        a = from_row(s, al * down(a, s), a)
        c = to_row(s, be * up(c, s), c)
        e = e + al * down(e, s) + be * up(e, s)
        s, k = 2 * s, k + 1
    re = 1.0 / e
    return a * re, c * re, re


def reduce_rhs(d, kept, re):
    n = d.shape[0]
    s, k = 1, 0
    while s < n:
        al, be = kept(k)
        if s % TILE == 0:
            zero = jnp.zeros_like(d[:s])
            d = (
                d
                + jnp.concatenate([zero, al[s:] * d[:-s]], axis=0)
                + jnp.concatenate([be[:-s] * d[s:], zero], axis=0)
            )
        else:
            d = d + al * down(d, s) + be * up(d, s)
        s, k = 2 * s, k + 1
    return d * re


def others(n, me):
    return [k + (me <= k).astype(jnp.int32) for k in range(n - 1)]


class Gather:
    def __init__(self, axis, n, me, buf, send, recv):
        targets = others(n, me)
        self.copies = [
            pltpu.make_async_remote_copy(buf.at[me], buf.at[me], send, recv, {axis: to}, MESH)
            for to in targets
        ]
        many = buf.at[pl.ds(0, n - 1)]
        self.all = pltpu.make_async_remote_copy(many, many, send, recv, {axis: targets[0]}, MESH)

    def start(self):
        for copy in self.copies:
            copy.start()

    def wait(self):
        self.all.wait_recv()

    def wait_sent(self):
        self.all.wait_send()


def put(buf, me, plies, q, p, v):
    buf[me, q * plies + p : q * plies + p + 1, :] = v


def put_responses(buf, me, plies, p, A, C):
    n = A.shape[0]
    for q, v in enumerate((A[:1], C[n - 1 :], A[n - 1 :])):
        put(buf, me, plies, q, p, v)


def flux_factor(ends, responses, n, plies):
    def of(buf, j, q):
        return buf[j, q * plies : (q + 1) * plies, :]

    w, m = [None] * (n + 1), [None] * (n + 1)
    cross = [of(responses, j, 2) for j in range(n)]
    for j in range(1, n):
        diag = 1.0 / (HALF_RATE * (of(ends, j - 1, 1) + of(ends, j, 0)))
        diag = diag + of(responses, j - 1, 1) + of(responses, j, 0)
        if j > 1:
            m[j] = cross[j - 1] * w[j - 1]
            diag = diag - cross[j - 1] * m[j]
        w[j] = 1.0 / diag
    return w, m, cross


def flux_solve(buf, n, plies, me, w, m, cross, fix=None):
    y = [None] * (n + 1)
    for j in range(1, n):
        r = buf[j - 1, plies : 2 * plies, :] - buf[j, :plies, :]
        if fix is not None:
            r = r + fix[j]
        y[j] = r if j == 1 else r + m[j] * y[j - 1]
    zero = jnp.zeros((plies, buf.shape[-1]), jnp.float32)
    top, bottom = zero, zero
    flux = None
    for j in range(n - 1, 0, -1):
        flux = w[j] * (y[j] if flux is None else y[j] + cross[j] * flux)
        top = jnp.where(me == j, flux, top)
        bottom = jnp.where(me + 1 == j, flux, bottom)
    return top, bottom


def kernel(
    ns, nc, plies, classes,
    pressure_hbm, fill_hbm, class_hbm, table_hbm, span_hbm, chord_hbm, rate_hbm,
    D_c, A_c, C_c, flux_ref,
    pressure, state, table_ref, inlet_ref, rate_ref, plane_ref, half, keep_s, keep_c, A_s, C_s, E_s, E_c, D,
    sides, near_out, near_in, cross_out, cross_in, ends_s, coef_s, coef_c, edge_c,
    sent, landed,
):
    rows, width = pressure.shape[1:]
    me_s, me_c = lax.axis_index("span"), lax.axis_index("chord")
    odd = lax.rem(me_c, 2)
    beside = me_c + 1 - 2 * odd
    across = lax.rem(me_c + nc - 1 + 2 * odd, nc)
    is_odd = odd == 1
    has_across = jnp.where(is_odd, me_c < nc - 1, me_c > 0)
    lane_beside = (1 - odd) * (width - 1)
    lane_across = odd * (width - 1)

    barrier = pltpu.get_barrier_semaphore()
    loads = [
        pltpu.make_async_copy(src, dst, sent.at[i])
        for src, dst, i in (
            (span_hbm, inlet_ref.at[0], 3), (chord_hbm, inlet_ref.at[1], 3), (rate_hbm, rate_ref, 4),
            (table_hbm, table_ref, 2), (class_hbm, state.at[0], 0), (fill_hbm, state.at[1], 0),
            (pressure_hbm, pressure, 1),
        )
    ]
    for load in loads:
        load.start()
    for o in range(1, nc):
        pl.semaphore_signal(
            barrier, inc=1, device_id={"chord": lax.rem(me_c + o, nc)}, device_id_type=MESH
        )
    for to in others(ns, me_s):
        pl.semaphore_signal(barrier, inc=1, device_id={"span": to}, device_id_type=MESH)
        pl.semaphore_signal(
            barrier, inc=1, device_id={"span": to, "chord": across}, device_id_type=MESH
        )

    pltpu.make_async_copy(inlet_ref, inlet_ref, sent.at[3]).wait()
    loads[2].wait()
    row_id = lax.broadcasted_iota(jnp.int32, (rows, rate_ref.shape[1]), 0) + me_s * rows
    col_id = lax.broadcasted_iota(jnp.int32, (width, rate_ref.shape[1]), 0) + me_c * width
    row_hits = jnp.where(row_id == inlet_ref[0], rate_ref[...], 0.0)
    col_hits = jnp.where(col_id == inlet_ref[1], 1.0, 0.0)
    plane_ref[...] = lax.dot_general(
        row_hits, col_hits, (((1,), (1,)), ((), ())),
        precision=lax.Precision.HIGHEST, preferred_element_type=jnp.float32,
    )
    loads[3].wait()
    pltpu.make_async_copy(state, state, sent.at[0]).wait()
    pltpu.make_async_copy(pressure, pressure, sent.at[1]).wait()

    conds, turned, fields = [], [], []
    for p in range(plies):
        perm = jnp.full((rows, width), table_ref[p, 0], jnp.float32)
        kl = state[0, p]
        for k in range(1, classes):
            perm = jnp.where(kl == k, table_ref[p, k], perm)
        st = state[1, p]
        cond = perm * jnp.where(st == 0, 1.0, jnp.where(st == 1, 0.5, 0.25))
        conds.append(cond)
        turned.append(cond.T)
        fields.append(pressure[p].T)
        for q, v in ((p, turned[p]), (plies + p, fields[p])):
            head, tail = v[:1], v[width - 1 :]
            near_out[q : q + 1, :] = jnp.where(is_odd, head, tail)
            cross_out[q : q + 1, :] = jnp.where(is_odd, tail, head)
            ends_s[me_s, 2 * plies + q : 2 * plies + q + 1, :] = jnp.where(is_odd, tail, head)
        for q, v in enumerate((cond[:1], cond[rows - 1 :])):
            put(ends_s, me_s, plies, q, p, v)
    pl.semaphore_wait(barrier, 2 * (ns - 1) + nc - 1)
    near = pltpu.make_async_remote_copy(
        near_out, near_in, sent.at[0], landed.at[0], {"chord": beside}, MESH
    )
    near.start()
    mine = pltpu.make_async_remote_copy(
        cross_out, cross_in.at[me_s], sent.at[1], landed.at[1], {"chord": across}, MESH
    )
    mine.start()
    for to in others(ns, me_s):
        pltpu.make_async_remote_copy(
            cross_out, cross_in.at[me_s], sent.at[1], landed.at[2], {"span": to, "chord": across}, MESH
        ).start()
    span_ends = Gather("span", ns, me_s, ends_s, sent.at[3], landed.at[4])
    span_ends.start()

    def keeper(ref, p):
        def keep(k, al, be):
            ref[k, 0, p] = al
            ref[k, 1, p] = be

        return keep

    def kept(ref, p):
        return lambda k: (ref[k, 0, p], ref[k, 1, p])

    for p in range(plies):
        A, C, re = factor(conds[p], keeper(keep_s, p))
        A_s[p], C_s[p], E_s[p] = A, C, re
        put_responses(coef_s, me_s, plies, p, A, C)
        for q, response in enumerate((A.T, C.T)):
            head, tail = response[:1], response[width - 1 :]
            put(coef_s, me_s, plies, 3 + q, p, jnp.where(is_odd, tail, head))
            sides[q, p : p + 1, :] = jnp.where(is_odd, head, tail)

    plane = plane_ref[...]
    for p in range(plies):
        f, other = fields[p], fields[plies - 1 - p]
        g = HALF_RATE * (turned[p] + up(turned[p], 1))
        flow = to_row(1, g * (up(f, 1) - f), jnp.zeros_like(f))
        back = from_row(1, down(flow, 1), jnp.zeros_like(f))
        rhs = (f + (flow - back) + COUPLE * (other - f)).T + plane
        half[p] = rhs
        put(coef_s, me_s, plies, 5, p, jnp.sum(A_s[p] * rhs, axis=0, keepdims=True))
        put(coef_s, me_s, plies, 6, p, jnp.sum(C_s[p] * rhs, axis=0, keepdims=True))
    near.wait_recv()
    near.wait_send()

    def inflow(ours, theirs):
        return (
            HALF_RATE
            * (theirs[:plies] + ours[:plies])
            * (theirs[plies : 2 * plies] - ours[plies : 2 * plies])
        )

    lane = lax.broadcasted_iota(jnp.int32, (plies, width), 1)
    from_beside = inflow(near_out[...], near_in[...])
    for q in range(2):
        change = jnp.sum(sides[q] * from_beside, axis=1, keepdims=True)
        coef_s[me_s, (5 + q) * plies : (6 + q) * plies, :] = (
            coef_s[me_s, (5 + q) * plies : (6 + q) * plies, :]
            + jnp.where(lane == lane_beside, change, 0.0)
        )
    span_coefs = Gather("span", ns, me_s, coef_s, sent.at[2], landed.at[3])
    span_coefs.start()

    for p in range(plies):
        A_c[p] = turned[p]

    @pl.when(me_c >= 0)
    def after_sending_span():
        for p in range(plies):
            cond = A_c[p]
            put(coef_c, me_c, plies, 3, p, cond[:1])
            put(coef_c, me_c, plies, 4, p, cond[width - 1 :])
            A, C, re = factor(cond, keeper(keep_c, p))
            A_c[p], C_c[p], E_c[p] = A, C, re
            put_responses(coef_c, me_c, plies, p, A, C)

    chord_coefs = Gather("chord", nc, me_c, coef_c, sent.at[4], landed.at[5])
    chord_coefs.start()

    mine.wait_recv()
    from_across = jnp.where(has_across, inflow(cross_out[...], cross_in[me_s]), 0.0)
    lanes = lax.broadcasted_iota(jnp.int32, (width, rows), 0)
    for p in range(plies):
        change = jnp.where(lanes == lane_beside, from_beside[p : p + 1], 0.0) + jnp.where(
            lanes == lane_across, from_across[p : p + 1], 0.0
        )
        rhs = half[p] + change.T
        half[p] = rhs
        D[p] = reduce_rhs(rhs, kept(keep_s, p), E_s[p])

    few = cross_in.at[pl.ds(0, ns - 1)]
    pltpu.make_async_remote_copy(few, few, sent.at[1], landed.at[2], {"chord": across}, MESH).wait_recv()
    span_ends.wait()
    span_coefs.wait()
    parts = flux_factor(ends_s, coef_s, ns, plies)
    by_first, by_last = [], []
    for i in range(ns):
        ours = ends_s[i, 2 * plies : 4 * plies, :]
        flow = jnp.where(has_across, inflow(ours, cross_in[i]), 0.0)
        by_first.append(jnp.sum(coef_s[i, 3 * plies : 4 * plies, :] * flow, axis=1, keepdims=True))
        by_last.append(jnp.sum(coef_s[i, 4 * plies : 5 * plies, :] * flow, axis=1, keepdims=True))
    fix = [None] + [
        jnp.where(lane == lane_across, by_last[i - 1] - by_first[i], 0.0) for i in range(1, ns)
    ]
    top, bottom = flux_solve(coef_s.at[:, pl.ds(5 * plies, 2 * plies)], ns, plies, me_s, *parts, fix)
    plane = plane_ref[...]
    stars = [D[p] + A_s[p] * top[p : p + 1] - C_s[p] * bottom[p : p + 1] for p in range(plies)]
    for p in range(plies):
        star, other = stars[p], stars[plies - 1 - p]
        second = (2.0 * star - half[p] + COUPLE * (other - star) + plane).T
        D_c[p] = second
        edge_c[me_c, p : p + 1, :] = jnp.sum(A_c[p] * second, axis=0, keepdims=True)
        edge_c[me_c, plies + p : plies + p + 1, :] = jnp.sum(C_c[p] * second, axis=0, keepdims=True)
    chord_edges = Gather("chord", nc, me_c, edge_c, sent.at[0], landed.at[6])
    chord_edges.start()

    @pl.when(me_c >= 0)
    def after_sending():
        for p in range(plies):
            D_c[p] = reduce_rhs(D_c[p], kept(keep_c, p), E_c[p])

    chord_coefs.wait()
    parts = flux_factor(coef_c.at[:, pl.ds(3 * plies, 2 * plies)], coef_c, nc, plies)
    pltpu.make_async_remote_copy(cross_in, cross_in, sent.at[1], landed.at[2], {"chord": across}, MESH).wait_send()
    for gather in (span_ends, span_coefs, chord_coefs):
        gather.wait_sent()
    chord_edges.wait()
    flux_ref[0], flux_ref[1] = flux_solve(edge_c, nc, plies, me_c, *parts)
    chord_edges.wait_sent()


def finish(plies, D_c, A_c, C_c, flux_ref, out_hbm, block, sem):
    for p in range(plies):
        top, bottom = flux_ref[0, p : p + 1, :], flux_ref[1, p : p + 1, :]
        block[p] = (D_c[p] + A_c[p] * top - C_c[p] * bottom).T
        pltpu.make_async_copy(block.at[p], out_hbm.at[p], sem.at[0]).start()
    pltpu.make_async_copy(block, out_hbm, sem.at[0]).wait()


def levels(n):
    return max(1, (n - 1).bit_length())


def per_device(ns, nc, pressure, fill_state, perm_class, perm_table, inlet_span, inlet_chord, inlet_rate):
    plies, rows, width = pressure.shape
    classes = perm_table.shape[1]
    inlets = inlet_span.shape[0]
    vmem = pl.BlockSpec(memory_space=pltpu.VMEM)
    hbm = pl.BlockSpec(memory_space=pltpu.HBM)
    f32 = jnp.float32
    block = pltpu.VMEM((plies, rows, width), f32)
    block_t = pltpu.VMEM((plies, width, rows), f32)
    dma = lambda n: pltpu.SemaphoreType.DMA((n,))
    lines = pltpu.VMEM((plies, width, rows), f32)
    solved = pl.pallas_call(
        functools.partial(kernel, ns, nc, plies, classes),
        out_shape=(lines, lines, lines, pltpu.VMEM((2, plies, rows), f32)),
        in_specs=[hbm] * 7,
        out_specs=(vmem,) * 4,
        scratch_shapes=[
            block, pltpu.VMEM((2, plies, rows, width), jnp.int32),
            pltpu.SMEM(perm_table.shape, f32),
            pltpu.VMEM((2, 1, inlets), jnp.int32), pltpu.VMEM((1, inlets), f32),
            pltpu.VMEM((rows, width), f32),
            block,
            pltpu.VMEM((levels(rows), 2, plies, rows, width), f32),
            pltpu.VMEM((levels(width), 2, plies, width, rows), f32),
            block, block, block, block_t, block,
            pltpu.VMEM((2, plies, rows), f32),
            pltpu.VMEM((2 * plies, rows), f32),
            pltpu.VMEM((2 * plies, rows), f32),
            pltpu.VMEM((2 * plies, rows), f32),
            pltpu.VMEM((ns, 2 * plies, rows), f32),
            pltpu.VMEM((ns, 4 * plies, width), f32),
            pltpu.VMEM((ns, 7 * plies, width), f32),
            pltpu.VMEM((nc, 5 * plies, rows), f32),
            pltpu.VMEM((nc, 2 * plies, rows), f32),
            dma(5), dma(7),
        ],
        compiler_params=pltpu.CompilerParams(collective_id=0, has_side_effects=True, vmem_limit_bytes=LIMIT),
    )(
        *(
            pltpu.with_memory_space_constraint(x, pltpu.HBM)
            for x in (
                pressure, fill_state, perm_class, perm_table, inlet_span.reshape(1, inlets),
                inlet_chord.reshape(1, inlets), inlet_rate.reshape(1, inlets),
            )
        )
    )
    return pl.pallas_call(
        functools.partial(finish, plies),
        out_shape=jax.ShapeDtypeStruct(pressure.shape, f32),
        in_specs=[vmem] * 4,
        out_specs=hbm,
        scratch_shapes=[block, dma(1)],
        compiler_params=pltpu.CompilerParams(vmem_limit_bytes=LIMIT),
    )(*solved)


def solution(mesh):
    block = P(None, "span", "chord")
    return jax.shard_map(
        functools.partial(per_device, mesh.shape["span"], mesh.shape["chord"]),
        mesh=mesh,
        in_specs=(block, block, block, P(), P(), P(), P()),
        out_specs=block,
        check_vma=False,
    )
```

```python
import functools

import jax
import jax.numpy as jnp
from jax import lax
from jax.experimental import pallas as pl
from jax.experimental.pallas import tpu as pltpu
from jax.sharding import PartitionSpec as P

HALF_RATE = 200.0
COUPLE = 0.3
MESH = pl.DeviceIdType.MESH
TILE = 8
LIMIT = 16 << 20


def down(x, s):
    if s % TILE == 0:
        return jnp.concatenate([x[-s:], x[:-s]], axis=0)
    return pltpu.roll(x, s, 0)


def up(x, s):
    if s % TILE == 0:
        return jnp.concatenate([x[s:], x[:s]], axis=0)
    return pltpu.roll(x, x.shape[0] - s, 0)


def from_row(s, value, other):
    if s % TILE == 0:
        return jnp.concatenate([other[:s], value[s:]], axis=0)
    rows = lax.broadcasted_iota(jnp.int32, value.shape, 0)
    return jnp.where(rows >= s, value, other)


def to_row(s, value, other):
    n = value.shape[0]
    if s % TILE == 0:
        return jnp.concatenate([value[: n - s], other[n - s :]], axis=0)
    rows = lax.broadcasted_iota(jnp.int32, value.shape, 0)
    return jnp.where(rows < n - s, value, other)


def faces(cond):
    return to_row(1, HALF_RATE * (cond + up(cond, 1)), jnp.zeros_like(cond))


def eliminate(a, c, e, keep):
    n = e.shape[0]
    zero = jnp.zeros_like(e)
    s, k = 1, 0
    while s < n:
        a_in = from_row(s, a, zero)
        c_in = to_row(s, c, zero)
        rb = 1.0 / (e + a_in + c_in)
        al = a_in * down(rb, s)
        be = c_in * up(rb, s)
        keep(k, al, be)
        a = from_row(s, al * down(a, s), a)
        c = to_row(s, be * up(c, s), c)
        e = e + al * down(e, s) + be * up(e, s)
        s, k = 2 * s, k + 1
    re = 1.0 / e
    return a * re, c * re, re


def factor(cond, keep):
    one = jnp.ones_like(cond)
    g = HALF_RATE * (cond + up(cond, 1))
    return eliminate(from_row(1, down(g, 1), one), to_row(1, g, one), one, keep)


def responses(conds, g_ref, e_ref, A_ref, C_ref):
    n, w = conds[0].shape
    count = len(conds)
    top = [jnp.ones((1, w), jnp.float32)] * count
    g_now, e_now = [faces(cond) for cond in conds], None
    steps = []
    while n > TILE:
        m = n // 2
        step = []
        for p in range(count):
            g_ref[p, :n, :] = g_now[p]
            if e_now is not None:
                e_ref[p, :n, :] = e_now[p]
        for p in range(count):
            g_even, g_odd = g_ref[p, pl.ds(0, m, 2), :], g_ref[p, pl.ds(1, m, 2), :]
            if e_now is None:
                e_even, e_odd = jnp.ones((m, w), jnp.float32), jnp.ones((m, w), jnp.float32)
            else:
                e_even, e_odd = e_ref[p, pl.ds(0, m, 2), :], e_ref[p, pl.ds(1, m, 2), :]
            before = down(g_odd, 1)
            zero = jnp.zeros_like(before)
            a = from_row(1, before, zero)
            rb = 1.0 / (e_even + a + g_even)
            P = from_row(1, before, jnp.broadcast_to(top[p], before.shape)) * rb
            Q = g_even * rb
            step.append((P, Q))
            top[p] = Q[:1] * top[p]
            g_now[p] = to_row(1, up(P * g_even, 1), zero)
            e_new = e_odd + Q * e_even + to_row(1, up(P * e_even, 1), zero)
            step[p] = (P, Q, e_new)
        e_now = [x[2] for x in step]
        steps.append((m, step))
        n = m
    lines = []
    for p in range(count):
        one = jnp.ones((n, w), jnp.float32)
        e = one if e_now is None else e_now[p]
        a = from_row(1, down(g_now[p], 1), jnp.broadcast_to(top[p], e.shape))
        lines.append(eliminate(a, to_row(1, g_now[p], one), e, lambda *x: None)[:2])
    for m, step in reversed(steps):
        for p in range(count):
            P, Q, _ = step[p]
            first, last = lines[p]
            A_ref[p, pl.ds(1, m, 2), :] = first
            C_ref[p, pl.ds(1, m, 2), :] = last
            A_ref[p, pl.ds(0, m, 2), :] = P * from_row(1, down(first, 1), jnp.ones_like(first)) + Q * first
            C_ref[p, pl.ds(0, m, 2), :] = P * from_row(1, down(last, 1), jnp.zeros_like(last)) + Q * last
        for p in range(count):
            lines[p] = (A_ref[p, : 2 * m, :], C_ref[p, : 2 * m, :])
    return lines


def reduce_rhs(d, kept, re):
    n = d.shape[0]
    s, k = 1, 0
    while s < n:
        al, be = kept(k)
        if s % TILE == 0:
            zero = jnp.zeros_like(d[:s])
            d = (
                d
                + jnp.concatenate([zero, al[s:] * d[:-s]], axis=0)
                + jnp.concatenate([be[:-s] * d[s:], zero], axis=0)
            )
        else:
            d = d + al * down(d, s) + be * up(d, s)
        s, k = 2 * s, k + 1
    return d * re


def others(n, me):
    return [k + (me <= k).astype(jnp.int32) for k in range(n - 1)]


class Gather:
    def __init__(self, axis, n, me, buf, send, recv):
        targets = others(n, me)
        self.copies = [
            pltpu.make_async_remote_copy(buf.at[me], buf.at[me], send, recv, {axis: to}, MESH)
            for to in targets
        ]
        many = buf.at[pl.ds(0, n - 1)]
        self.all = pltpu.make_async_remote_copy(many, many, send, recv, {axis: targets[0]}, MESH)

    def start(self):
        for copy in self.copies:
            copy.start()

    def wait(self):
        self.all.wait_recv()

    def wait_sent(self):
        self.all.wait_send()


def put(buf, me, plies, q, p, v):
    buf[me, q * plies + p : q * plies + p + 1, :] = v


def put_responses(buf, me, plies, p, A, C):
    n = A.shape[0]
    for q, v in enumerate((A[:1], C[n - 1 :], A[n - 1 :])):
        put(buf, me, plies, q, p, v)


def flux_factor(ends, responses, n, plies):
    def of(buf, j, q):
        return buf[j, q * plies : (q + 1) * plies, :]

    w, m = [None] * (n + 1), [None] * (n + 1)
    cross = [of(responses, j, 2) for j in range(n)]
    for j in range(1, n):
        diag = 1.0 / (HALF_RATE * (of(ends, j - 1, 1) + of(ends, j, 0)))
        diag = diag + of(responses, j - 1, 1) + of(responses, j, 0)
        if j > 1:
            m[j] = cross[j - 1] * w[j - 1]
            diag = diag - cross[j - 1] * m[j]
        w[j] = 1.0 / diag
    return w, m, cross


def flux_solve(buf, n, plies, me, w, m, cross, fix=None):
    y = [None] * (n + 1)
    for j in range(1, n):
        r = buf[j - 1, plies : 2 * plies, :] - buf[j, :plies, :]
        if fix is not None:
            r = r + fix[j]
        y[j] = r if j == 1 else r + m[j] * y[j - 1]
    zero = jnp.zeros((plies, buf.shape[-1]), jnp.float32)
    top, bottom = zero, zero
    flux = None
    for j in range(n - 1, 0, -1):
        flux = w[j] * (y[j] if flux is None else y[j] + cross[j] * flux)
        top = jnp.where(me == j, flux, top)
        bottom = jnp.where(me + 1 == j, flux, bottom)
    return top, bottom


def kernel(
    ns, nc, plies, classes,
    pressure_hbm, fill_hbm, class_hbm, table_hbm, span_hbm, chord_hbm, rate_hbm,
    D_c, A_c, C_c, flux_ref,
    pressure, state, table_ref, inlet_ref, rate_ref, plane_ref, half, keep_s, keep_c, g_ref, e_ref, A_s, C_s, E_s, E_c, D,
    sides, near_out, near_in, cross_out, cross_in, ends_s, coef_s, coef_c, edge_c,
    sent, landed,
):
    rows, width = pressure.shape[1:]
    me_s, me_c = lax.axis_index("span"), lax.axis_index("chord")
    odd = lax.rem(me_c, 2)
    beside = me_c + 1 - 2 * odd
    across = lax.rem(me_c + nc - 1 + 2 * odd, nc)
    is_odd = odd == 1
    has_across = jnp.where(is_odd, me_c < nc - 1, me_c > 0)
    lane_beside = (1 - odd) * (width - 1)
    lane_across = odd * (width - 1)

    barrier = pltpu.get_barrier_semaphore()
    loads = [
        pltpu.make_async_copy(src, dst, sent.at[i])
        for src, dst, i in (
            (span_hbm, inlet_ref.at[0], 3), (chord_hbm, inlet_ref.at[1], 3), (rate_hbm, rate_ref, 4),
            (table_hbm, table_ref, 2), (class_hbm, state.at[0], 0), (fill_hbm, state.at[1], 0),
            (pressure_hbm, pressure, 1),
        )
    ]
    for load in loads:
        load.start()
    for o in range(1, nc):
        pl.semaphore_signal(
            barrier, inc=1, device_id={"chord": lax.rem(me_c + o, nc)}, device_id_type=MESH
        )
    for to in others(ns, me_s):
        pl.semaphore_signal(barrier, inc=1, device_id={"span": to}, device_id_type=MESH)
        pl.semaphore_signal(
            barrier, inc=1, device_id={"span": to, "chord": across}, device_id_type=MESH
        )

    pltpu.make_async_copy(inlet_ref, inlet_ref, sent.at[3]).wait()
    loads[2].wait()
    row_id = lax.broadcasted_iota(jnp.int32, (rows, rate_ref.shape[1]), 0) + me_s * rows
    col_id = lax.broadcasted_iota(jnp.int32, (width, rate_ref.shape[1]), 0) + me_c * width
    row_hits = jnp.where(row_id == inlet_ref[0], rate_ref[...], 0.0)
    col_hits = jnp.where(col_id == inlet_ref[1], 1.0, 0.0)
    plane_ref[...] = lax.dot_general(
        row_hits, col_hits, (((1,), (1,)), ((), ())),
        precision=lax.Precision.HIGHEST, preferred_element_type=jnp.float32,
    )
    loads[3].wait()
    pltpu.make_async_copy(state, state, sent.at[0]).wait()
    pltpu.make_async_copy(pressure, pressure, sent.at[1]).wait()

    conds, turned, fields = [], [], []
    for p in range(plies):
        perm = jnp.full((rows, width), table_ref[p, 0], jnp.float32)
        kl = state[0, p]
        for k in range(1, classes):
            perm = jnp.where(kl == k, table_ref[p, k], perm)
        st = state[1, p]
        cond = perm * jnp.where(st == 0, 1.0, jnp.where(st == 1, 0.5, 0.25))
        conds.append(cond)
        turned.append(cond.T)
        fields.append(pressure[p].T)
        for q, v in ((p, turned[p]), (plies + p, fields[p])):
            head, tail = v[:1], v[width - 1 :]
            near_out[q : q + 1, :] = jnp.where(is_odd, head, tail)
            cross_out[q : q + 1, :] = jnp.where(is_odd, tail, head)
            ends_s[me_s, 2 * plies + q : 2 * plies + q + 1, :] = jnp.where(is_odd, tail, head)
        for q, v in enumerate((cond[:1], cond[rows - 1 :])):
            put(ends_s, me_s, plies, q, p, v)
    pl.semaphore_wait(barrier, 2 * (ns - 1) + nc - 1)
    near = pltpu.make_async_remote_copy(
        near_out, near_in, sent.at[0], landed.at[0], {"chord": beside}, MESH
    )
    near.start()
    mine = pltpu.make_async_remote_copy(
        cross_out, cross_in.at[me_s], sent.at[1], landed.at[1], {"chord": across}, MESH
    )
    mine.start()
    for to in others(ns, me_s):
        pltpu.make_async_remote_copy(
            cross_out, cross_in.at[me_s], sent.at[1], landed.at[2], {"span": to, "chord": across}, MESH
        ).start()
    span_ends = Gather("span", ns, me_s, ends_s, sent.at[3], landed.at[4])
    span_ends.start()

    def keeper(ref, p):
        def keep(k, al, be):
            ref[k, 0, p] = al
            ref[k, 1, p] = be

        return keep

    def kept(ref, p):
        return lambda k: (ref[k, 0, p], ref[k, 1, p])

    for p, (A, C) in enumerate(responses(conds, g_ref, e_ref, A_s, C_s)):
        put_responses(coef_s, me_s, plies, p, A, C)
        for q, response in enumerate((A.T, C.T)):
            head, tail = response[:1], response[width - 1 :]
            put(coef_s, me_s, plies, 3 + q, p, jnp.where(is_odd, tail, head))
            sides[q, p : p + 1, :] = jnp.where(is_odd, head, tail)

    plane = plane_ref[...]
    for p in range(plies):
        f, other = fields[p], fields[plies - 1 - p]
        g = HALF_RATE * (turned[p] + up(turned[p], 1))
        flow = to_row(1, g * (up(f, 1) - f), jnp.zeros_like(f))
        back = from_row(1, down(flow, 1), jnp.zeros_like(f))
        rhs = (f + (flow - back) + COUPLE * (other - f)).T + plane
        half[p] = rhs
        put(coef_s, me_s, plies, 5, p, jnp.sum(A_s[p] * rhs, axis=0, keepdims=True))
        put(coef_s, me_s, plies, 6, p, jnp.sum(C_s[p] * rhs, axis=0, keepdims=True))
    near.wait_recv()

    def inflow(ours, theirs):
        return (
            HALF_RATE
            * (theirs[:plies] + ours[:plies])
            * (theirs[plies : 2 * plies] - ours[plies : 2 * plies])
        )

    lane = lax.broadcasted_iota(jnp.int32, (plies, width), 1)
    from_beside = inflow(near_out[...], near_in[...])
    for q in range(2):
        change = jnp.sum(sides[q] * from_beside, axis=1, keepdims=True)
        coef_s[me_s, (5 + q) * plies : (6 + q) * plies, :] = (
            coef_s[me_s, (5 + q) * plies : (6 + q) * plies, :]
            + jnp.where(lane == lane_beside, change, 0.0)
        )
    span_coefs = Gather("span", ns, me_s, coef_s, sent.at[2], landed.at[3])
    span_coefs.start()

    for p in range(plies):
        A_c[p] = turned[p]
        D[p] = conds[p]

    @pl.when(me_c >= 0)
    def after_sending_span():
        for p in range(plies):
            E_s[p] = factor(D[p], keeper(keep_s, p))[2]
        for p in range(plies):
            cond = A_c[p]
            put(coef_c, me_c, plies, 3, p, cond[:1])
            put(coef_c, me_c, plies, 4, p, cond[width - 1 :])
            A, C, re = factor(cond, keeper(keep_c, p))
            A_c[p], C_c[p], E_c[p] = A, C, re
            put_responses(coef_c, me_c, plies, p, A, C)

    chord_coefs = Gather("chord", nc, me_c, coef_c, sent.at[4], landed.at[5])
    chord_coefs.start()

    near.wait_send()
    mine.wait_recv()
    from_across = jnp.where(has_across, inflow(cross_out[...], cross_in[me_s]), 0.0)
    lanes = lax.broadcasted_iota(jnp.int32, (width, rows), 0)
    for p in range(plies):
        change = jnp.where(lanes == lane_beside, from_beside[p : p + 1], 0.0) + jnp.where(
            lanes == lane_across, from_across[p : p + 1], 0.0
        )
        rhs = half[p] + change.T
        half[p] = rhs
        D[p] = reduce_rhs(rhs, kept(keep_s, p), E_s[p])

    few = cross_in.at[pl.ds(0, ns - 1)]
    pltpu.make_async_remote_copy(few, few, sent.at[1], landed.at[2], {"chord": across}, MESH).wait_recv()
    span_ends.wait()
    span_coefs.wait()
    parts = flux_factor(ends_s, coef_s, ns, plies)
    by_first, by_last = [], []
    for i in range(ns):
        ours = ends_s[i, 2 * plies : 4 * plies, :]
        flow = jnp.where(has_across, inflow(ours, cross_in[i]), 0.0)
        by_first.append(jnp.sum(coef_s[i, 3 * plies : 4 * plies, :] * flow, axis=1, keepdims=True))
        by_last.append(jnp.sum(coef_s[i, 4 * plies : 5 * plies, :] * flow, axis=1, keepdims=True))
    fix = [None] + [
        jnp.where(lane == lane_across, by_last[i - 1] - by_first[i], 0.0) for i in range(1, ns)
    ]
    top, bottom = flux_solve(coef_s.at[:, pl.ds(5 * plies, 2 * plies)], ns, plies, me_s, *parts, fix)
    plane = plane_ref[...]
    stars = [D[p] + A_s[p] * top[p : p + 1] - C_s[p] * bottom[p : p + 1] for p in range(plies)]
    for p in range(plies):
        star, other = stars[p], stars[plies - 1 - p]
        second = (2.0 * star - half[p] + COUPLE * (other - star) + plane).T
        D_c[p] = second
        edge_c[me_c, p : p + 1, :] = jnp.sum(A_c[p] * second, axis=0, keepdims=True)
        edge_c[me_c, plies + p : plies + p + 1, :] = jnp.sum(C_c[p] * second, axis=0, keepdims=True)
    chord_edges = Gather("chord", nc, me_c, edge_c, sent.at[0], landed.at[6])
    chord_edges.start()

    @pl.when(me_c >= 0)
    def after_sending():
        for p in range(plies):
            D_c[p] = reduce_rhs(D_c[p], kept(keep_c, p), E_c[p])

    chord_coefs.wait()
    parts = flux_factor(coef_c.at[:, pl.ds(3 * plies, 2 * plies)], coef_c, nc, plies)
    pltpu.make_async_remote_copy(cross_in, cross_in, sent.at[1], landed.at[2], {"chord": across}, MESH).wait_send()
    for gather in (span_ends, span_coefs, chord_coefs):
        gather.wait_sent()
    chord_edges.wait()
    flux_ref[0], flux_ref[1] = flux_solve(edge_c, nc, plies, me_c, *parts)
    chord_edges.wait_sent()


def finish(plies, D_c, A_c, C_c, flux_ref, out_hbm, block, sem):
    for p in range(plies):
        top, bottom = flux_ref[0, p : p + 1, :], flux_ref[1, p : p + 1, :]
        block[p] = (D_c[p] + A_c[p] * top - C_c[p] * bottom).T
        pltpu.make_async_copy(block.at[p], out_hbm.at[p], sem.at[0]).start()
    pltpu.make_async_copy(block, out_hbm, sem.at[0]).wait()


def levels(n):
    return max(1, (n - 1).bit_length())


def per_device(ns, nc, pressure, fill_state, perm_class, perm_table, inlet_span, inlet_chord, inlet_rate):
    plies, rows, width = pressure.shape
    classes = perm_table.shape[1]
    inlets = inlet_span.shape[0]
    vmem = pl.BlockSpec(memory_space=pltpu.VMEM)
    hbm = pl.BlockSpec(memory_space=pltpu.HBM)
    f32 = jnp.float32
    block = pltpu.VMEM((plies, rows, width), f32)
    block_t = pltpu.VMEM((plies, width, rows), f32)
    dma = lambda n: pltpu.SemaphoreType.DMA((n,))
    lines = pltpu.VMEM((plies, width, rows), f32)
    solved = pl.pallas_call(
        functools.partial(kernel, ns, nc, plies, classes),
        out_shape=(lines, lines, lines, pltpu.VMEM((2, plies, rows), f32)),
        in_specs=[hbm] * 7,
        out_specs=(vmem,) * 4,
        scratch_shapes=[
            block, pltpu.VMEM((2, plies, rows, width), jnp.int32),
            pltpu.SMEM(perm_table.shape, f32),
            pltpu.VMEM((2, 1, inlets), jnp.int32), pltpu.VMEM((1, inlets), f32),
            pltpu.VMEM((rows, width), f32),
            block,
            pltpu.VMEM((levels(rows), 2, plies, rows, width), f32),
            pltpu.VMEM((levels(width), 2, plies, width, rows), f32),
            block, block,
            block, block, block, block_t, block,
            pltpu.VMEM((2, plies, rows), f32),
            pltpu.VMEM((2 * plies, rows), f32),
            pltpu.VMEM((2 * plies, rows), f32),
            pltpu.VMEM((2 * plies, rows), f32),
            pltpu.VMEM((ns, 2 * plies, rows), f32),
            pltpu.VMEM((ns, 4 * plies, width), f32),
            pltpu.VMEM((ns, 7 * plies, width), f32),
            pltpu.VMEM((nc, 5 * plies, rows), f32),
            pltpu.VMEM((nc, 2 * plies, rows), f32),
            dma(5), dma(7),
        ],
        compiler_params=pltpu.CompilerParams(collective_id=0, has_side_effects=True, vmem_limit_bytes=LIMIT),
    )(
        *(
            pltpu.with_memory_space_constraint(x, pltpu.HBM)
            for x in (
                pressure, fill_state, perm_class, perm_table, inlet_span.reshape(1, inlets),
                inlet_chord.reshape(1, inlets), inlet_rate.reshape(1, inlets),
            )
        )
    )
    return pl.pallas_call(
        functools.partial(finish, plies),
        out_shape=jax.ShapeDtypeStruct(pressure.shape, f32),
        in_specs=[vmem] * 4,
        out_specs=hbm,
        scratch_shapes=[block, dma(1)],
        compiler_params=pltpu.CompilerParams(vmem_limit_bytes=LIMIT),
    )(*solved)


def solution(mesh):
    block = P(None, "span", "chord")
    return jax.shard_map(
        functools.partial(per_device, mesh.shape["span"], mesh.shape["chord"]),
        mesh=mesh,
        in_specs=(block, block, block, P(), P(), P(), P()),
        out_specs=block,
        check_vma=False,
    )
```

```python
import functools

import jax
import jax.numpy as jnp
from jax import lax
from jax.experimental import pallas as pl
from jax.experimental.pallas import tpu as pltpu
from jax.sharding import PartitionSpec as P

HALF_RATE = 200.0
COUPLE = 0.3
MESH = pl.DeviceIdType.MESH
TILE = 8
LIMIT = 16 << 20


def down(x, s):
    if s % TILE == 0:
        return jnp.concatenate([x[-s:], x[:-s]], axis=0)
    return pltpu.roll(x, s, 0)


def up(x, s):
    if s % TILE == 0:
        return jnp.concatenate([x[s:], x[:s]], axis=0)
    return pltpu.roll(x, x.shape[0] - s, 0)


def from_row(s, value, other):
    if s % TILE == 0:
        return jnp.concatenate([other[:s], value[s:]], axis=0)
    rows = lax.broadcasted_iota(jnp.int32, value.shape, 0)
    return jnp.where(rows >= s, value, other)


def to_row(s, value, other):
    n = value.shape[0]
    if s % TILE == 0:
        return jnp.concatenate([value[: n - s], other[n - s :]], axis=0)
    rows = lax.broadcasted_iota(jnp.int32, value.shape, 0)
    return jnp.where(rows < n - s, value, other)


def faces(cond):
    return to_row(1, HALF_RATE * (cond + up(cond, 1)), jnp.zeros_like(cond))


def eliminate(a, c, e, keep):
    n = e.shape[0]
    zero = jnp.zeros_like(e)
    s, k = 1, 0
    while s < n:
        a_in = from_row(s, a, zero)
        c_in = to_row(s, c, zero)
        rb = 1.0 / (e + a_in + c_in)
        al = a_in * down(rb, s)
        be = c_in * up(rb, s)
        keep(k, al, be)
        a = from_row(s, al * down(a, s), a)
        c = to_row(s, be * up(c, s), c)
        e = e + al * down(e, s) + be * up(e, s)
        s, k = 2 * s, k + 1
    re = 1.0 / e
    return a * re, c * re, re


def factor(cond, keep):
    one = jnp.ones_like(cond)
    g = HALF_RATE * (cond + up(cond, 1))
    return eliminate(from_row(1, down(g, 1), one), to_row(1, g, one), one, keep)


def responses(conds, g_ref, e_ref, A_ref, C_ref):
    n, w = conds[0].shape
    count = len(conds)
    top = [jnp.ones((1, w), jnp.float32)] * count
    g_now, e_now = [faces(cond) for cond in conds], None
    steps = []
    while n > TILE:
        m = n // 2
        step = []
        for p in range(count):
            g_ref[p, :n, :] = g_now[p]
            if e_now is not None:
                e_ref[p, :n, :] = e_now[p]
        for p in range(count):
            g_even, g_odd = g_ref[p, pl.ds(0, m, 2), :], g_ref[p, pl.ds(1, m, 2), :]
            if e_now is None:
                e_even, e_odd = jnp.ones((m, w), jnp.float32), jnp.ones((m, w), jnp.float32)
            else:
                e_even, e_odd = e_ref[p, pl.ds(0, m, 2), :], e_ref[p, pl.ds(1, m, 2), :]
            before = down(g_odd, 1)
            zero = jnp.zeros_like(before)
            a = from_row(1, before, zero)
            rb = 1.0 / (e_even + a + g_even)
            P = from_row(1, before, jnp.broadcast_to(top[p], before.shape)) * rb
            Q = g_even * rb
            step.append((P, Q))
            top[p] = Q[:1] * top[p]
            g_now[p] = to_row(1, up(P * g_even, 1), zero)
            e_new = e_odd + Q * e_even + to_row(1, up(P * e_even, 1), zero)
            step[p] = (P, Q, e_new)
        e_now = [x[2] for x in step]
        steps.append((m, step))
        n = m
    lines = []
    for p in range(count):
        one = jnp.ones((n, w), jnp.float32)
        e = one if e_now is None else e_now[p]
        a = from_row(1, down(g_now[p], 1), jnp.broadcast_to(top[p], e.shape))
        lines.append(eliminate(a, to_row(1, g_now[p], one), e, lambda *x: None)[:2])
    for m, step in reversed(steps):
        for p in range(count):
            P, Q, _ = step[p]
            first, last = lines[p]
            A_ref[p, pl.ds(1, m, 2), :] = first
            C_ref[p, pl.ds(1, m, 2), :] = last
            A_ref[p, pl.ds(0, m, 2), :] = P * from_row(1, down(first, 1), jnp.ones_like(first)) + Q * first
            C_ref[p, pl.ds(0, m, 2), :] = P * from_row(1, down(last, 1), jnp.zeros_like(last)) + Q * last
        for p in range(count):
            lines[p] = (A_ref[p, : 2 * m, :], C_ref[p, : 2 * m, :])
    return lines


def reduce_rhs(d, kept, re):
    n = d.shape[0]
    s, k = 1, 0
    while s < n:
        al, be = kept(k)
        if s % TILE == 0:
            zero = jnp.zeros_like(d[:s])
            d = (
                d
                + jnp.concatenate([zero, al[s:] * d[:-s]], axis=0)
                + jnp.concatenate([be[:-s] * d[s:], zero], axis=0)
            )
        else:
            d = d + al * down(d, s) + be * up(d, s)
        s, k = 2 * s, k + 1
    return d * re


def others(n, me):
    return [k + (me <= k).astype(jnp.int32) for k in range(n - 1)]


class Gather:
    def __init__(self, axis, n, me, buf, send, recv):
        targets = others(n, me)
        self.copies = [
            pltpu.make_async_remote_copy(buf.at[me], buf.at[me], send, recv, {axis: to}, MESH)
            for to in targets
        ]
        many = buf.at[pl.ds(0, n - 1)]
        self.all = pltpu.make_async_remote_copy(many, many, send, recv, {axis: targets[0]}, MESH)

    def start(self):
        for copy in self.copies:
            copy.start()

    def wait(self):
        self.all.wait_recv()

    def wait_sent(self):
        self.all.wait_send()


def put(buf, me, plies, q, p, v):
    buf[me, q * plies + p : q * plies + p + 1, :] = v


def put_responses(buf, me, plies, p, A, C):
    n = A.shape[0]
    for q, v in enumerate((A[:1], C[n - 1 :], A[n - 1 :])):
        put(buf, me, plies, q, p, v)


def of(buf, j, q, plies):
    return buf[j, q * plies : (q + 1) * plies, :]


def face_gaps(ends, n, plies):
    return [None] + [
        1.0 / (HALF_RATE * (of(ends, j - 1, 1, plies) + of(ends, j, 0, plies))) for j in range(1, n)
    ]


def flux_factor(gaps, responses, n, plies):
    w, m = [None] * (n + 1), [None] * (n + 1)
    cross = [of(responses, j, 2, plies) for j in range(n)]
    for j in range(1, n):
        diag = gaps[j] + of(responses, j - 1, 1, plies) + of(responses, j, 0, plies)
        if j > 1:
            m[j] = cross[j - 1] * w[j - 1]
            diag = diag - cross[j - 1] * m[j]
        w[j] = 1.0 / diag
    return w, m, cross


def flux_solve(buf, n, plies, me, w, m, cross, fix=None):
    y = [None] * (n + 1)
    for j in range(1, n):
        r = buf[j - 1, plies : 2 * plies, :] - buf[j, :plies, :]
        if fix is not None:
            r = r + fix[j]
        y[j] = r if j == 1 else r + m[j] * y[j - 1]
    zero = jnp.zeros((plies, buf.shape[-1]), jnp.float32)
    top, bottom = zero, zero
    flux = None
    for j in range(n - 1, 0, -1):
        flux = w[j] * (y[j] if flux is None else y[j] + cross[j] * flux)
        top = jnp.where(me == j, flux, top)
        bottom = jnp.where(me + 1 == j, flux, bottom)
    return top, bottom


def kernel(
    ns, nc, plies, classes,
    pressure_hbm, fill_hbm, class_hbm, table_hbm, span_hbm, chord_hbm, rate_hbm,
    D_c, A_c, C_c, flux_ref,
    pressure, state, table_ref, inlet_ref, rate_ref, plane_ref, half, keep_s, keep_c, g_ref, e_ref, A_s, C_s, E_s, E_c, D,
    sides, near_out, near_in, cross_out, cross_in, ends_s, coef_s, coef_c, edge_c,
    sent, landed,
):
    rows, width = pressure.shape[1:]
    me_s, me_c = lax.axis_index("span"), lax.axis_index("chord")
    odd = lax.rem(me_c, 2)
    beside = me_c + 1 - 2 * odd
    across = lax.rem(me_c + nc - 1 + 2 * odd, nc)
    is_odd = odd == 1
    has_across = jnp.where(is_odd, me_c < nc - 1, me_c > 0)
    lane_beside = (1 - odd) * (width - 1)
    lane_across = odd * (width - 1)

    barrier = pltpu.get_barrier_semaphore()
    pairs = [
        (span_hbm, inlet_ref.at[0], plies + 2), (chord_hbm, inlet_ref.at[1], plies + 2),
        (rate_hbm, rate_ref, plies + 3), (table_hbm, table_ref, plies + 1),
    ]
    for p in range(plies):
        pairs.append((class_hbm.at[p], state.at[p, 0], p))
        pairs.append((fill_hbm.at[p], state.at[p, 1], p))
        if p == 0:
            pairs.append((pressure_hbm, pressure, plies))
    loads = [pltpu.make_async_copy(src, dst, sent.at[i]) for src, dst, i in pairs]
    for load in loads:
        load.start()
    for o in range(1, nc):
        pl.semaphore_signal(
            barrier, inc=1, device_id={"chord": lax.rem(me_c + o, nc)}, device_id_type=MESH
        )
    for to in others(ns, me_s):
        pl.semaphore_signal(barrier, inc=1, device_id={"span": to}, device_id_type=MESH)
        pl.semaphore_signal(
            barrier, inc=1, device_id={"span": to, "chord": across}, device_id_type=MESH
        )

    pltpu.make_async_copy(inlet_ref, inlet_ref, sent.at[plies + 2]).wait()
    loads[2].wait()
    row_id = lax.broadcasted_iota(jnp.int32, (rows, rate_ref.shape[1]), 0) + me_s * rows
    col_id = lax.broadcasted_iota(jnp.int32, (width, rate_ref.shape[1]), 0) + me_c * width
    row_hits = jnp.where(row_id == inlet_ref[0], rate_ref[...], 0.0)
    col_hits = jnp.where(col_id == inlet_ref[1], 1.0, 0.0)
    plane_ref[...] = lax.dot_general(
        row_hits, col_hits, (((1,), (1,)), ((), ())),
        precision=lax.Precision.HIGHEST, preferred_element_type=jnp.float32,
    )
    loads[3].wait()

    conds, turned, fields = [], [], []
    for p in range(plies):
        pltpu.make_async_copy(state.at[p], state.at[p], sent.at[p]).wait()
        if p == 0:
            loads[6].wait()
        perm = jnp.full((rows, width), table_ref[p, 0], jnp.float32)
        kl = state[p, 0]
        for k in range(1, classes):
            perm = jnp.where(kl == k, table_ref[p, k], perm)
        st = state[p, 1]
        cond = perm * jnp.where(st == 0, 1.0, jnp.where(st == 1, 0.5, 0.25))
        conds.append(cond)
        turned.append(cond.T)
        fields.append(pressure[p].T)
        for q, v in ((p, turned[p]), (plies + p, fields[p])):
            head, tail = v[:1], v[width - 1 :]
            near_out[q : q + 1, :] = jnp.where(is_odd, head, tail)
            cross_out[q : q + 1, :] = jnp.where(is_odd, tail, head)
            ends_s[me_s, 2 * plies + q : 2 * plies + q + 1, :] = jnp.where(is_odd, tail, head)
        for q, v in enumerate((cond[:1], cond[rows - 1 :])):
            put(ends_s, me_s, plies, q, p, v)
    pl.semaphore_wait(barrier, 2 * (ns - 1) + nc - 1)
    near = pltpu.make_async_remote_copy(
        near_out, near_in, sent.at[0], landed.at[0], {"chord": beside}, MESH
    )
    near.start()
    mine = pltpu.make_async_remote_copy(
        cross_out, cross_in.at[me_s], sent.at[1], landed.at[1], {"chord": across}, MESH
    )
    mine.start()
    for to in others(ns, me_s):
        pltpu.make_async_remote_copy(
            cross_out, cross_in.at[me_s], sent.at[1], landed.at[2], {"span": to, "chord": across}, MESH
        ).start()
    span_ends = Gather("span", ns, me_s, ends_s, sent.at[3], landed.at[4])
    span_ends.start()

    def keeper(ref, p):
        def keep(k, al, be):
            ref[k, 0, p] = al
            ref[k, 1, p] = be

        return keep

    def kept(ref, p):
        return lambda k: (ref[k, 0, p], ref[k, 1, p])

    for p, (A, C) in enumerate(responses(conds, g_ref, e_ref, A_s, C_s)):
        put_responses(coef_s, me_s, plies, p, A, C)
        for q, response in enumerate((A.T, C.T)):
            head, tail = response[:1], response[width - 1 :]
            put(coef_s, me_s, plies, 3 + q, p, jnp.where(is_odd, tail, head))
            sides[q, p : p + 1, :] = jnp.where(is_odd, head, tail)

    plane = plane_ref[...]
    for p in range(plies):
        f, other = fields[p], fields[plies - 1 - p]
        g = HALF_RATE * (turned[p] + up(turned[p], 1))
        flow = to_row(1, g * (up(f, 1) - f), jnp.zeros_like(f))
        back = from_row(1, down(flow, 1), jnp.zeros_like(f))
        rhs = (f + (flow - back) + COUPLE * (other - f)).T + plane
        half[p] = rhs
        put(coef_s, me_s, plies, 5, p, jnp.sum(A_s[p] * rhs, axis=0, keepdims=True))
        put(coef_s, me_s, plies, 6, p, jnp.sum(C_s[p] * rhs, axis=0, keepdims=True))
    near.wait_recv()

    def inflow(ours, theirs):
        return (
            HALF_RATE
            * (theirs[:plies] + ours[:plies])
            * (theirs[plies : 2 * plies] - ours[plies : 2 * plies])
        )

    lane = lax.broadcasted_iota(jnp.int32, (plies, width), 1)
    from_beside = inflow(near_out[...], near_in[...])
    for q in range(2):
        change = jnp.sum(sides[q] * from_beside, axis=1, keepdims=True)
        coef_s[me_s, (5 + q) * plies : (6 + q) * plies, :] = (
            coef_s[me_s, (5 + q) * plies : (6 + q) * plies, :]
            + jnp.where(lane == lane_beside, change, 0.0)
        )
    span_coefs = Gather("span", ns, me_s, coef_s, sent.at[2], landed.at[3])
    span_coefs.start()

    for p in range(plies):
        A_c[p] = turned[p]
        D[p] = conds[p]

    @pl.when(me_c >= 0)
    def after_sending_span():
        for p in range(plies):
            E_s[p] = factor(D[p], keeper(keep_s, p))[2]
        for p in range(plies):
            cond = A_c[p]
            put(coef_c, me_c, plies, 3, p, cond[:1])
            put(coef_c, me_c, plies, 4, p, cond[width - 1 :])
            A, C, re = factor(cond, keeper(keep_c, p))
            A_c[p], C_c[p], E_c[p] = A, C, re
            put_responses(coef_c, me_c, plies, p, A, C)

    chord_coefs = Gather("chord", nc, me_c, coef_c, sent.at[4], landed.at[5])
    chord_coefs.start()

    near.wait_send()
    mine.wait_recv()
    from_across = jnp.where(has_across, inflow(cross_out[...], cross_in[me_s]), 0.0)
    lanes = lax.broadcasted_iota(jnp.int32, (width, rows), 0)
    for p in range(plies):
        change = jnp.where(lanes == lane_beside, from_beside[p : p + 1], 0.0) + jnp.where(
            lanes == lane_across, from_across[p : p + 1], 0.0
        )
        rhs = half[p] + change.T
        half[p] = rhs
        D[p] = reduce_rhs(rhs, kept(keep_s, p), E_s[p])
    for p in range(plies):
        star, other = D[p], D[plies - 1 - p]
        half[p] = 2.0 * star - half[p] + COUPLE * (other - star) + plane_ref[...]

    few = cross_in.at[pl.ds(0, ns - 1)]
    pltpu.make_async_remote_copy(few, few, sent.at[1], landed.at[2], {"chord": across}, MESH).wait_recv()
    span_ends.wait()
    flows = [
        jnp.where(has_across, inflow(ends_s[i, 2 * plies : 4 * plies, :], cross_in[i]), 0.0)
        for i in range(ns)
    ]
    gaps = face_gaps(ends_s, ns, plies)
    span_coefs.wait()
    parts = flux_factor(gaps, coef_s, ns, plies)
    by_first, by_last = [], []
    for i in range(ns):
        flow = flows[i]
        by_first.append(jnp.sum(coef_s[i, 3 * plies : 4 * plies, :] * flow, axis=1, keepdims=True))
        by_last.append(jnp.sum(coef_s[i, 4 * plies : 5 * plies, :] * flow, axis=1, keepdims=True))
    fix = [None] + [
        jnp.where(lane == lane_across, by_last[i - 1] - by_first[i], 0.0) for i in range(1, ns)
    ]
    top, bottom = flux_solve(coef_s.at[:, pl.ds(5 * plies, 2 * plies)], ns, plies, me_s, *parts, fix)
    gains = [A_s[p] * top[p : p + 1] - C_s[p] * bottom[p : p + 1] for p in range(plies)]
    for p in range(plies):
        star, other = gains[p], gains[plies - 1 - p]
        second = (half[p] + ((2.0 - COUPLE) * star + COUPLE * other)).T
        D_c[p] = second
        edge_c[me_c, p : p + 1, :] = jnp.sum(A_c[p] * second, axis=0, keepdims=True)
        edge_c[me_c, plies + p : plies + p + 1, :] = jnp.sum(C_c[p] * second, axis=0, keepdims=True)
    chord_edges = Gather("chord", nc, me_c, edge_c, sent.at[5], landed.at[6])
    chord_edges.start()

    @pl.when(me_c >= 0)
    def after_sending():
        for p in range(plies):
            D_c[p] = reduce_rhs(D_c[p], kept(keep_c, p), E_c[p])

    chord_coefs.wait()
    parts = flux_factor(face_gaps(coef_c.at[:, pl.ds(3 * plies, 2 * plies)], nc, plies), coef_c, nc, plies)
    pltpu.make_async_remote_copy(cross_in, cross_in, sent.at[1], landed.at[2], {"chord": across}, MESH).wait_send()
    for gather in (span_ends, span_coefs, chord_coefs):
        gather.wait_sent()
    chord_edges.wait()
    flux_ref[0], flux_ref[1] = flux_solve(edge_c, nc, plies, me_c, *parts)
    chord_edges.wait_sent()


def finish(plies, D_c, A_c, C_c, flux_ref, out_hbm, block, sem):
    for p in range(plies):
        top, bottom = flux_ref[0, p : p + 1, :], flux_ref[1, p : p + 1, :]
        block[p] = (D_c[p] + A_c[p] * top - C_c[p] * bottom).T
        pltpu.make_async_copy(block.at[p], out_hbm.at[p], sem.at[0]).start()
    pltpu.make_async_copy(block, out_hbm, sem.at[0]).wait()


def levels(n):
    return max(1, (n - 1).bit_length())


def per_device(ns, nc, pressure, fill_state, perm_class, perm_table, inlet_span, inlet_chord, inlet_rate):
    plies, rows, width = pressure.shape
    classes = perm_table.shape[1]
    inlets = inlet_span.shape[0]
    vmem = pl.BlockSpec(memory_space=pltpu.VMEM)
    hbm = pl.BlockSpec(memory_space=pltpu.HBM)
    f32 = jnp.float32
    block = pltpu.VMEM((plies, rows, width), f32)
    block_t = pltpu.VMEM((plies, width, rows), f32)
    dma = lambda n: pltpu.SemaphoreType.DMA((n,))
    lines = pltpu.VMEM((plies, width, rows), f32)
    solved = pl.pallas_call(
        functools.partial(kernel, ns, nc, plies, classes),
        out_shape=(lines, lines, lines, pltpu.VMEM((2, plies, rows), f32)),
        in_specs=[hbm] * 7,
        out_specs=(vmem,) * 4,
        scratch_shapes=[
            block, pltpu.VMEM((plies, 2, rows, width), jnp.int32),
            pltpu.SMEM(perm_table.shape, f32),
            pltpu.VMEM((2, 1, inlets), jnp.int32), pltpu.VMEM((1, inlets), f32),
            pltpu.VMEM((rows, width), f32),
            block,
            pltpu.VMEM((levels(rows), 2, plies, rows, width), f32),
            pltpu.VMEM((levels(width), 2, plies, width, rows), f32),
            block, block,
            block, block, block, block_t, block,
            pltpu.VMEM((2, plies, rows), f32),
            pltpu.VMEM((2 * plies, rows), f32),
            pltpu.VMEM((2 * plies, rows), f32),
            pltpu.VMEM((2 * plies, rows), f32),
            pltpu.VMEM((ns, 2 * plies, rows), f32),
            pltpu.VMEM((ns, 4 * plies, width), f32),
            pltpu.VMEM((ns, 7 * plies, width), f32),
            pltpu.VMEM((nc, 5 * plies, rows), f32),
            pltpu.VMEM((nc, 2 * plies, rows), f32),
            dma(max(6, plies + 4)), dma(7),
        ],
        compiler_params=pltpu.CompilerParams(collective_id=0, has_side_effects=True, vmem_limit_bytes=LIMIT),
    )(
        *(
            pltpu.with_memory_space_constraint(x, pltpu.HBM)
            for x in (
                pressure, fill_state, perm_class, perm_table, inlet_span.reshape(1, inlets),
                inlet_chord.reshape(1, inlets), inlet_rate.reshape(1, inlets),
            )
        )
    )
    return pl.pallas_call(
        functools.partial(finish, plies),
        out_shape=jax.ShapeDtypeStruct(pressure.shape, f32),
        in_specs=[vmem] * 4,
        out_specs=hbm,
        scratch_shapes=[block, dma(1)],
        compiler_params=pltpu.CompilerParams(vmem_limit_bytes=LIMIT),
    )(*solved)


def solution(mesh):
    block = P(None, "span", "chord")
    return jax.shard_map(
        functools.partial(per_device, mesh.shape["span"], mesh.shape["chord"]),
        mesh=mesh,
        in_specs=(block, block, block, P(), P(), P(), P()),
        out_specs=block,
        check_vma=False,
    )
```
